32 devices in a mesh: dp: 8 (over y, x, core), fsdp: 4 (over z).
Axes of the slice: x: 2, y: 2, z: 4, core: 2. Of those that a mesh axis runs over, the one named last changes fastest.
Arguments:
- inputs: bfloat16 [32768, 960], P(('dp', 'fsdp')), may hold values from -6 to 6
- w_query: bfloat16 [960, 960], P('fsdp'), may hold values from -0.1875 to 0.1875
- w_key: bfloat16 [960, 320], P('fsdp'), may hold values from -0.1875 to 0.1875
- w_value: bfloat16 [960, 320], P('fsdp'), may hold values from -0.1875 to 0.1875
- w_out: bfloat16 [960, 960], P('fsdp'), may hold values from -1 to 1
- w_gate: bfloat16 [960, 2560], P('fsdp'), may hold values from -0.1875 to 0.1875
- w_up: bfloat16 [960, 2560], P('fsdp'), may hold values from -0.1875 to 0.1875
- w_down: bfloat16 [2560, 960], P('fsdp'), may hold values from -0.125 to 0.125
- gain_attn: bfloat16 [960], P('fsdp'), may hold values from 0.5 to 1.5
- gain_ffn: bfloat16 [960], P('fsdp'), may hold values from 0.5 to 1.5
- w_router: bfloat16 [960, 3], P('fsdp'), may hold values from -0.125 to 0.125
- seq_start: int32 [32768], P(('dp', 'fsdp')), may hold values from 0 to 768, as said below
- pick_first: int32 [24576], P(('dp', 'fsdp')), may hold values from 0 to 1023, as said below
- pick_second: int32 [16384], P(('dp', 'fsdp')), may hold values from 0 to 1023, as said below
- pick_third: int32 [8192], P(('dp', 'fsdp')), may hold values from 0 to 1023, as said below
- out_grad: bfloat16 [32768, 960], P(('dp', 'fsdp')), may hold values from -6 to 6
Outputs:
- hidden_out: bfloat16 [32768, 960], P(('dp', 'fsdp'))
- grad_inputs: bfloat16 [32768, 960], P(('dp', 'fsdp'))
- grad_query: float32 [960, 960], P('fsdp')
- grad_key: float32 [960, 320], P('fsdp')
- grad_value: float32 [960, 320], P('fsdp')
- grad_out: float32 [960, 960], P('fsdp')
- grad_gate: float32 [960, 2560], P('fsdp')
- grad_up: float32 [960, 2560], P('fsdp')
- grad_down: float32 [2560, 960], P('fsdp')
- grad_gain_attn: float32 [960], P('fsdp')
- grad_gain_ffn: float32 [960], P('fsdp')
- grad_router: float32 [960, 3], P('fsdp')
The draws below stay inside these ranges and needn't reach their ends.
Inputs may be any that keep to these rules, and one draw needn't show every extreme that they name: Within each group of 1024 tokens either all tokens form one sequence (seq_start 0) or four sequences of 256 tokens; a third of the groups, rounded down, hold one sequence. `pick_first`: per group, 768 distinct ascending indices below 1024. `pick_second`: per group, 512 distinct ascending indices, all among the group's pick_first. `pick_third`: per group, 256 distinct ascending indices, all among the group's pick_second.
All inputs are finite; a program needn't handle non-finite values.
Results may differ from the reference program's by a relative error of at most 0.025.
Values may be sent and summed in bfloat16 or wider, within the bound.
A program may use at most 256 MiB of HBM per device.

```python
import math
import jax
import jax.numpy as jnp
from jax import lax

D = 960
HEADS = 15
KV_HEADS = 5
HEAD_DIM = 64
FF = 2560
NREC = 3
TOK_DEV = 1024
K1 = 768
K2 = 512
K3 = 256
NDEV = 32
TOKENS = 32768


def device_kinds(key):
    shuffled = jax.random.permutation(jax.random.fold_in(key, 11), NDEV)
    return shuffled < max(NDEV // 3, 1)


def token_ranks(key):
    subkeys = jax.random.split(jax.random.fold_in(key, 23), NDEV)
    orders = jax.vmap(lambda subkey: jax.random.permutation(subkey, TOK_DEV))(subkeys)
    scores = orders.astype(jnp.int32) + 2
    places = jnp.arange(TOK_DEV, dtype=jnp.int32)
    groups = jnp.arange(NDEV, dtype=jnp.int32)
    first_group = groups[:, None] == 0
    scores = jnp.where(first_group & (places[None, :] == 0), 0, scores)
    scores = jnp.where(first_group & (places[None, :] == TOK_DEV - 1), 1, scores)
    return jnp.argsort(jnp.argsort(scores, axis=1, stable=True), axis=1, stable=True)


def chosen_tokens(key, picked_count):
    ranks = token_ranks(key)
    outside = (ranks >= picked_count).astype(jnp.int32)
    picked = jnp.argsort(outside, axis=1, stable=True)[:, :picked_count]
    return picked.astype(jnp.int32).reshape(NDEV * picked_count)


def draw_seq_start(key, part):
    whole_device = device_kinds(key)
    places = jnp.arange(TOK_DEV, dtype=jnp.int32)
    short_start = places // (TOK_DEV // 4) * (TOK_DEV // 4)
    starts = jnp.where(whole_device[:, None], 0, short_start[None, :])
    return starts.astype(jnp.int32).reshape(NDEV * TOK_DEV)


def draw_pick_first(key, part):
    return chosen_tokens(key, K1)


def draw_pick_second(key, part):
    return chosen_tokens(key, K2)


def draw_pick_third(key, part):
    return chosen_tokens(key, K3)


def level_of(key, extent, pieces, low, high):
    loudness, own = 1.0, jax.random.fold_in(key, 6)
    for position, blocks in pieces:
        heights = jnp.exp(jax.random.uniform(jax.random.fold_in(own, position), (blocks,), jnp.float32, low / len(pieces), high / len(pieces)))
        loudness = loudness * jnp.repeat(heights, extent[position] // blocks).reshape([-1 if axis == position else 1 for axis in range(len(extent))])
    return loudness


def normal_values(key, shape, spread, bound, pieces=(), kind=jnp.bfloat16):
    values = jax.random.normal(key, shape, jnp.float32) * spread
    if len(pieces) > 0:
        values = level_of(key, shape, pieces, -0.22, 0.18) * values
    return jnp.clip(values, min=-bound, max=bound).astype(kind)


def setup_inputs(seed: int = 0) -> dict:
    arg_keys = jax.random.split(jax.random.key(seed), 17)
    inputs = normal_values(arg_keys[0], (TOKENS, D), 1.0, 6.0, ((0, 32),))
    w_query = normal_values(arg_keys[1], (D, D), D ** -0.5, 0.1875, ((0, 4),))
    w_key = normal_values(arg_keys[2], (D, KV_HEADS * HEAD_DIM), D ** -0.5, 0.1875, ((0, 4),))
    w_value = normal_values(arg_keys[3], (D, KV_HEADS * HEAD_DIM), D ** -0.5, 0.1875, ((0, 4),))
    w_out = normal_values(arg_keys[4], (D, D), (max(D // 32, 1)) ** -0.5, 1.0, ((0, 4),))
    w_gate = normal_values(arg_keys[5], (D, FF), D ** -0.5, 0.1875, ((0, 4),))
    w_up = normal_values(arg_keys[6], (D, FF), D ** -0.5, 0.1875, ((0, 4),))
    w_down = normal_values(arg_keys[7], (FF, D), FF ** -0.5, 0.125, ((0, 4),))
    gain_attn = jnp.clip(1.0 + 0.1 * jax.random.normal(arg_keys[8], (D,), jnp.float32), 0.5, 1.5).astype(jnp.bfloat16)
    gain_ffn = jnp.clip(1.0 + 0.1 * jax.random.normal(arg_keys[9], (D,), jnp.float32), 0.5, 1.5).astype(jnp.bfloat16)
    w_router = normal_values(arg_keys[10], (D, NREC), (2 * D) ** -0.5, 0.125, ((0, 4),))
    seq_start = draw_seq_start(jax.random.fold_in(arg_keys[16], 71), 0)
    pick_first = draw_pick_first(jax.random.fold_in(arg_keys[16], 71), 0)
    pick_second = draw_pick_second(jax.random.fold_in(arg_keys[16], 71), 0)
    pick_third = draw_pick_third(jax.random.fold_in(arg_keys[16], 71), 0)
    out_grad = normal_values(arg_keys[15], (TOKENS, D), 1.0, 6.0, ((0, 32),))
    return dict(inputs=inputs, w_query=w_query, w_key=w_key, w_value=w_value, w_out=w_out, w_gate=w_gate, w_up=w_up, w_down=w_down, gain_attn=gain_attn, gain_ffn=gain_ffn, w_router=w_router, seq_start=seq_start, pick_first=pick_first, pick_second=pick_second, pick_third=pick_third, out_grad=out_grad)


norm_eps = 1e-05
masked_score = -1e+30
highest = lax.Precision.HIGHEST

@jax.custom_vjp
def low(v):
    return lax.optimization_barrier(v.astype(jnp.bfloat16)).astype(jnp.float32)

@jax.custom_vjp
def low_back(v):
    return v

def low_keep(v):
    return (low(v), None)

def low_pass(kept, grad):
    return (grad,)

def back_keep(v):
    return (v, None)

def back_low(kept, grad):
    return (low(grad),)
low.defvjp(low_keep, low_pass)
low_back.defvjp(back_keep, back_low)

def product(left, right):
    return jnp.dot(left, right, precision=highest, preferred_element_type=jnp.float32)

def rms_norm(values, gain):
    return values * lax.rsqrt(lax.optimization_barrier(jnp.mean(values * values, axis=-1, keepdims=True)) + norm_eps) * gain

def rotary(values, positions, head_count):
    half_dim = HEAD_DIM // 2
    frequency = jnp.exp(jnp.arange(half_dim, dtype=jnp.float32) * (-2.0 * math.log(10000.0) / HEAD_DIM))
    angles = positions.astype(jnp.float32)[:, None] * frequency[None, :]
    cosine_table = jnp.cos(angles)[:, None, :]
    sine_table = jnp.sin(angles)[:, None, :]
    shaped = values.reshape(values.shape[0], head_count, HEAD_DIM)
    first_half = shaped[..., :half_dim]
    second_half = shaped[..., half_dim:]
    turned = jnp.concatenate([first_half * cosine_table - second_half * sine_table, second_half * cosine_table + first_half * sine_table], axis=-1)
    return turned.reshape(values.shape[0], head_count * HEAD_DIM)

def attend(queries, keys_turned, values, allowed):
    row_count = queries.shape[0]
    group_size = HEADS // KV_HEADS
    query_groups = queries.reshape(row_count, KV_HEADS, group_size, HEAD_DIM).transpose(1, 2, 0, 3)
    key_groups = keys_turned.reshape(row_count, KV_HEADS, HEAD_DIM).transpose(1, 0, 2)
    value_groups = values.reshape(row_count, KV_HEADS, HEAD_DIM).transpose(1, 0, 2)
    score_scale = 1.0 / math.sqrt(HEAD_DIM)

    def one_group(operands):
        query_head, key_head, value_head = operands
        raw_scores = jnp.einsum('gqd,kd->gqk', query_head, key_head, precision=highest)
        scores = jnp.where(allowed[None], low_back(raw_scores * score_scale), masked_score)
        top_score = lax.optimization_barrier(jnp.max(scores, axis=-1, keepdims=True))
        weights = jnp.exp(scores - top_score)
        probabilities = weights / lax.optimization_barrier(jnp.sum(weights, axis=-1, keepdims=True))
        return jnp.einsum('gqk,kd->gqd', low(probabilities), value_head, precision=highest)
    mixed = lax.map(jax.checkpoint(one_group), (query_groups, key_groups, value_groups))
    return mixed.transpose(2, 0, 1, 3).reshape(row_count, HEADS * HEAD_DIM)

def device_forward(hidden, starts, pick_lists, weights):
    w_query, w_key, w_value, w_out, w_gate, w_up, w_down, gain_attn, gain_ffn, w_router = weights
    for section in range(NREC):
        token_index = pick_lists[section]
        token_rows = hidden[token_index]
        begins = starts[token_index]
        positions = token_index - begins
        allowed = (token_index[None, :] <= token_index[:, None]) & (begins[:, None] <= token_index[None, :])
        normed = low(rms_norm(token_rows, gain_attn))
        queries = low(rotary(low_back(product(normed, w_query)), positions, HEADS))
        keys_turned = low(rotary(low_back(product(normed, w_key)), positions, KV_HEADS))
        values = low(low_back(product(normed, w_value)))
        mixed = low(low_back(attend(queries, keys_turned, values, allowed)))
        attn_branch = low_back(product(mixed, w_out))
        inner = low(rms_norm(token_rows + attn_branch, gain_ffn))
        gate_pre = low_back(product(inner, w_gate))
        up_pre = low_back(product(inner, w_up))
        activated = low(gate_pre * jax.nn.sigmoid(gate_pre) * up_pre)
        ffn_branch = low_back(product(activated, w_down))
        router_gate = jax.nn.sigmoid(product(token_rows, w_router[:, section]))
        hidden = hidden.at[token_index].set(token_rows + router_gate[:, None] * (attn_branch + ffn_branch))
    return hidden

def reference(inputs, w_query, w_key, w_value, w_out, w_gate, w_up, w_down, gain_attn, gain_ffn, w_router, seq_start, pick_first, pick_second, pick_third, out_grad):
    weights = tuple((member.astype(jnp.float32) for member in (w_query, w_key, w_value, w_out, w_gate, w_up, w_down, gain_attn, gain_ffn, w_router)))
    starts = seq_start.reshape(NDEV, TOK_DEV)
    first_rows = pick_first.reshape(NDEV, K1)
    second_rows = pick_second.reshape(NDEV, K2)
    third_rows = pick_third.reshape(NDEV, K3)

    def forward(start_hidden, weight_tuple):
        blocks = start_hidden.reshape(NDEV, TOK_DEV, start_hidden.shape[1])

        def one_block(block, begin_row, first_pick, second_pick, third_pick):
            return device_forward(block, begin_row, (first_pick, second_pick, third_pick), weight_tuple)
        checked = jax.checkpoint(one_block)

        def scan_step(unused_carry, operands):
            return (unused_carry, checked(operands[0], operands[1], operands[2], operands[3], operands[4]))
        _, outcome = lax.scan(scan_step, (), (blocks, starts, first_rows, second_rows, third_rows))
        return outcome.reshape(start_hidden.shape)
    result, pullback = jax.vjp(forward, inputs.astype(jnp.float32), weights)
    grad_in, grad_weights = pullback(out_grad.astype(jnp.float32))
    return (result.astype(jnp.bfloat16), grad_in.astype(jnp.bfloat16), grad_weights[0], grad_weights[1], grad_weights[2], grad_weights[3], grad_weights[4], grad_weights[5], grad_weights[6], grad_weights[7], grad_weights[8], grad_weights[9])
```

```python
import functools
import math

import jax
import jax.numpy as jnp
from jax import lax
from jax.experimental import pallas as pl
from jax.experimental.pallas import tpu as pltpu
from jax.sharding import PartitionSpec as P

HEADS = 15
KV_HEADS = 5
HEAD_DIM = 64
HALF = HEAD_DIM // 2
GROUP = HEADS // KV_HEADS
NREC = 3
ROWS = 256

norm_eps = 1e-05
masked_score = -1e30
highest = lax.Precision.HIGHEST
f32 = jnp.float32
bf16 = jnp.bfloat16


def dot(spec, left, right):
    return jnp.einsum(spec, left, right, preferred_element_type=f32)


def swap_halves(x):
    return jnp.concatenate([x[:, HALF:], x[:, :HALF]], axis=1)


def matmul(a, b, dims):
    return lax.dot_general(a, b, (dims, ((), ())), preferred_element_type=f32)


QW = HEADS * HEAD_DIM
KW = KV_HEADS * HEAD_DIM


def attend_fwd_kernel(qkv_ref, cos_ref, sin_ref, cols_ref, rows_ref, o_ref, q_ref, k_ref, v_ref, lse_ref, bias, stats):
    step = pl.program_id(0)
    rows = pl.ds(pl.multiple_of(step * ROWS, ROWS), ROWS)

    @pl.when(step == 0)
    def _():
        cos, sin = cos_ref[...], sin_ref[...]
        for g in range(KV_HEADS):
            raw = qkv_ref[:, QW + g * HEAD_DIM : QW + (g + 1) * HEAD_DIM]
            k_ref[g] = (raw * cos + swap_halves(raw) * sin).astype(bf16)
            v_ref[g] = qkv_ref[:, QW + KW + g * HEAD_DIM : QW + KW + (g + 1) * HEAD_DIM].astype(bf16)

    cols = cols_ref[rows, :]
    token, begin = cols[:, 0:1], cols[:, 1:2]
    key_token = rows_ref[0:1, :]
    bias[...] = jnp.where((key_token <= token) & (key_token >= begin), 0.0, masked_score)
    cos, sin = cos_ref[rows, :], sin_ref[rows, :]
    stats[...] = jnp.zeros_like(stats)
    for n in range(HEADS):
        g = n // GROUP
        raw = qkv_ref[rows, n * HEAD_DIM : (n + 1) * HEAD_DIM]
        q = ((raw * cos + swap_halves(raw) * sin).astype(bf16).astype(f32) * (1.0 / math.sqrt(HEAD_DIM))).astype(bf16)
        q_ref[n, rows, :] = q
        s = matmul(q, k_ref[g], ((1,), (1,))) + bias[...]
        m = jnp.max(s, axis=1, keepdims=True)
        p = jnp.exp(s - m)
        t = jnp.sum(p, axis=1, keepdims=True)
        p = (p * (1.0 / t)).astype(bf16)
        o_ref[rows, n * HEAD_DIM : (n + 1) * HEAD_DIM] = matmul(p, v_ref[g], ((1,), (0,))).astype(bf16)
        stats[:, n : n + 1] = m + jnp.log(t)
    lse_ref[...] = jnp.transpose(stats[...])[:16]


def attend_fwd(qkv, cos, sin, cols, rows):
    k = qkv.shape[0]
    whole = lambda *shape: pl.BlockSpec(shape, lambda i: (0,) * len(shape))
    return pl.pallas_call(
        attend_fwd_kernel,
        grid=(k // ROWS,),
        out_shape=(
            jax.ShapeDtypeStruct((k, QW), bf16),
            jax.ShapeDtypeStruct((HEADS, k, HEAD_DIM), bf16),
            jax.ShapeDtypeStruct((KV_HEADS, k, HEAD_DIM), bf16),
            jax.ShapeDtypeStruct((KV_HEADS, k, HEAD_DIM), bf16),
            jax.ShapeDtypeStruct((16, k), f32),
        ),
        in_specs=[
            whole(k, QW + 2 * KW),
            whole(k, HEAD_DIM),
            whole(k, HEAD_DIM),
            whole(k, 2),
            whole(2, k),
        ],
        out_specs=(
            whole(k, QW),
            whole(HEADS, k, HEAD_DIM),
            whole(KV_HEADS, k, HEAD_DIM),
            whole(KV_HEADS, k, HEAD_DIM),
            pl.BlockSpec((16, ROWS), lambda i: (0, i)),
        ),
        scratch_shapes=[pltpu.VMEM((ROWS, k), f32), pltpu.VMEM((ROWS, 128), f32)],
        compiler_params=pltpu.CompilerParams(vmem_limit_bytes=56 << 20),
        name="attend_fwd",
    )(qkv, cos, sin, cols, rows)


def attend_bwd_kernel(
    q_ref, k_ref, v_ref, lse_ref, do_ref, cos_ref, sin_ref, cols_ref, rows_ref, out_ref, bias, dk, dv, kt
):
    step = pl.program_id(0)
    start = pl.multiple_of(step * ROWS, ROWS)
    rows = pl.ds(start, ROWS)

    @pl.when(step == 0)
    def _():
        dk[...] = jnp.zeros_like(dk)
        dv[...] = jnp.zeros_like(dv)
        for g in range(KV_HEADS):
            kt[g] = jnp.transpose(k_ref[g].astype(f32)).astype(bf16)

    key_token = cols_ref[:, 0:1]
    token, begin = rows_ref[0:1, pl.ds(start, ROWS)], rows_ref[1:2, pl.ds(start, ROWS)]
    bias[...] = jnp.where((key_token <= token) & (key_token >= begin), 0.0, masked_score)
    cos, sin = cos_ref[rows, :], sin_ref[rows, :]
    for n in range(HEADS):
        g = n // GROUP
        q = q_ref[n, rows, :]
        do = do_ref[rows, n * HEAD_DIM : (n + 1) * HEAD_DIM]
        s = matmul(k_ref[g], q, ((1,), (1,))) + bias[...]
        p = jnp.exp(s - lse_ref[n : n + 1, :])
        dp = matmul(v_ref[g], do, ((1,), (1,)))
        dv[g] += matmul(p.astype(bf16), do, ((1,), (0,)))
        pd = p * dp
        ds = (pd - p * jnp.sum(pd, axis=0, keepdims=True)).astype(bf16)
        dk[g] += matmul(ds, q, ((1,), (0,)))
        dq = jnp.transpose(matmul(kt[g], ds, ((1,), (0,)))) * (1.0 / math.sqrt(HEAD_DIM))
        out_ref[rows, n * HEAD_DIM : (n + 1) * HEAD_DIM] = (dq * cos - swap_halves(dq) * sin).astype(bf16)

    @pl.when(step == pl.num_programs(0) - 1)
    def _():
        cos, sin = cos_ref[...], sin_ref[...]
        for g in range(KV_HEADS):
            grad = dk[g]
            out_ref[:, QW + g * HEAD_DIM : QW + (g + 1) * HEAD_DIM] = (
                grad * cos - swap_halves(grad) * sin
            ).astype(bf16)
            out_ref[:, QW + KW + g * HEAD_DIM : QW + KW + (g + 1) * HEAD_DIM] = dv[g].astype(bf16)


def attend_bwd(q, k, v, lse, grad, cos, sin, cols, rows):
    count = grad.shape[0]
    whole = lambda *shape: pl.BlockSpec(shape, lambda i: (0,) * len(shape))
    return pl.pallas_call(
        attend_bwd_kernel,
        grid=(count // ROWS,),
        out_shape=jax.ShapeDtypeStruct((count, QW + 2 * KW), bf16),
        in_specs=[
            whole(HEADS, count, HEAD_DIM),
            whole(KV_HEADS, count, HEAD_DIM),
            whole(KV_HEADS, count, HEAD_DIM),
            pl.BlockSpec((16, ROWS), lambda i: (0, i)),
            whole(count, QW),
            whole(count, HEAD_DIM),
            whole(count, HEAD_DIM),
            whole(count, 2),
            whole(2, count),
        ],
        out_specs=whole(count, QW + 2 * KW),
        scratch_shapes=[
            pltpu.VMEM((count, ROWS), f32),
            pltpu.VMEM((KV_HEADS, count, HEAD_DIM), f32),
            pltpu.VMEM((KV_HEADS, count, HEAD_DIM), f32),
            pltpu.VMEM((KV_HEADS, HEAD_DIM, count), bf16),
        ],
        compiler_params=pltpu.CompilerParams(vmem_limit_bytes=56 << 20),
        name="attend_bwd",
    )(q, k, v, lse, grad, cos, sin, cols, rows)


def inverse_rms(values):
    return lax.rsqrt(jnp.mean(values * values, axis=-1, keepdims=True) + norm_eps)


def norm_back(values, gain, grad):
    scale = inverse_rms(values)
    unit = values * scale
    grad_unit = grad * gain
    grad_values = (grad_unit - unit * jnp.mean(grad_unit * unit, axis=-1, keepdims=True)) * scale
    return grad_values, jnp.sum(grad * unit, axis=0)


def forward_step(rows_in, tables, weights, section):
    wqkv, wo, wg, wu, wd, gain_attn, gain_ffn, router = weights
    normed = (rows_in * inverse_rms(rows_in) * gain_attn).astype(bf16)
    qkv = dot("kd,de->ke", normed, wqkv)
    mixed, q, k, v, lse = attend_fwd(qkv, *tables)
    attn = dot("ke,ed->kd", mixed, wo)
    middle = rows_in + attn
    inner = (middle * inverse_rms(middle) * gain_ffn).astype(bf16)
    gate = dot("kd,df->kf", inner, wg)
    up = dot("kd,df->kf", inner, wu)
    activated = (gate * jax.nn.sigmoid(gate) * up).astype(bf16)
    ffn = dot("kf,fd->kd", activated, wd)
    gate_c = jax.nn.sigmoid(jnp.sum(rows_in * router[:, section][None, :], axis=1, keepdims=True))
    branches = attn + ffn
    out = rows_in + gate_c * branches
    kept = (rows_in, normed, q, k, v, lse, mixed, middle, inner, gate.astype(bf16), up.astype(bf16), activated, gate_c, branches)
    return out, kept


def backward_step(grad_new, kept, tables, weights, section):
    wqkv, wo, wg, wu, wd, gain_attn, gain_ffn, router = weights
    rows_in, normed, q, k, v, lse, mixed, middle, inner, gate, up, activated, gate_c, branches = kept
    gate, up = gate.astype(f32), up.astype(f32)
    dz = jnp.sum(grad_new * branches, axis=1, keepdims=True) * gate_c * (1.0 - gate_c)
    router_grad = jnp.sum(rows_in * dz, axis=0)
    grad_rows = grad_new + dz * router[:, section][None, :]
    grad_branch = gate_c * grad_new
    grad_ffn = grad_branch.astype(bf16)
    grad_act = dot("kd,fd->kf", grad_ffn, wd)
    sig = jax.nn.sigmoid(gate)
    grad_gate = (grad_act * up * (sig + gate * sig * (1.0 - sig))).astype(bf16)
    grad_up = (grad_act * (gate * sig)).astype(bf16)
    grad_inner = dot("kf,df->kd", grad_gate, wg) + dot("kf,df->kd", grad_up, wu)
    grad_middle, gain_ffn_grad = norm_back(middle, gain_ffn, grad_inner)
    grad_attn = (grad_branch + grad_middle).astype(bf16)
    grad_mixed = dot("kd,ed->ke", grad_attn, wo).astype(bf16)
    grad_qkv = attend_bwd(q, k, v, lse, grad_mixed, *tables)
    grad_normed = dot("ke,de->kd", grad_qkv, wqkv)
    grad_norm_rows, gain_attn_grad = norm_back(rows_in, gain_attn, grad_normed)
    grad_rows = grad_rows + grad_middle + grad_norm_rows
    pairs = ((activated, grad_ffn), (inner, grad_gate), (inner, grad_up), (mixed, grad_attn), (normed, grad_qkv))
    return grad_rows, pairs, (gain_attn_grad, gain_ffn_grad, router_grad)


def gather_all(shard):
    if shard.shape[0] % lax.axis_size("dp"):
        return lax.all_gather(shard, "fsdp", axis=0, tiled=True)
    rows = shard.shape[0] // lax.axis_size("dp")
    part = lax.dynamic_slice_in_dim(shard, lax.axis_index("dp") * rows, rows, 0)
    return lax.all_gather(part, ("fsdp", "dp"), axis=0, tiled=True)


def reduce_all(total):
    chunks = lax.axis_size("dp") * lax.axis_size("fsdp")
    if total.shape[0] % chunks:
        part = lax.psum_scatter(total, "fsdp", scatter_dimension=0, tiled=True)
        return lax.psum(part, "dp")
    rows = total.shape[0] // chunks
    padded = jnp.pad(total.reshape(chunks, rows, -1), ((0, 0), (0, -rows % 16), (0, 0)))
    part = lax.psum_scatter(padded.reshape(-1, total.shape[1]), ("fsdp", "dp"), scatter_dimension=0, tiled=True)[:rows]
    return lax.all_gather(part, "dp", axis=0, tiled=True)


def body(
    inputs, w_query, w_key, w_value, w_out, w_gate, w_up, w_down, gain_attn, gain_ffn, w_router,
    seq_start, pick_first, pick_second, pick_third, out_grad,
):
    picks = (pick_first, pick_second, pick_third)
    counts = tuple(p.shape[0] for p in picks)
    tokens = inputs.shape[0]

    gathered1 = gather_all(jnp.concatenate([w_out, w_query, w_key, w_value], axis=1))
    wg, wu, wd = gather_all(w_gate), gather_all(w_up), gather_all(w_down)
    wo, wqkv = gathered1[:, :QW], gathered1[:, QW:]
    small = jnp.concatenate([gain_attn[:, None], gain_ffn[:, None], w_router], axis=1)
    small = lax.all_gather(small, "fsdp", axis=0, tiled=True).astype(f32)
    weights = (wqkv, wo, wg, wu, wd, small[:, 0], small[:, 1], small[:, 2:5])

    places = jnp.arange(tokens, dtype=jnp.int32)
    level = jnp.full((tokens,), NREC, jnp.int32)
    for p in picks:
        level = level - jnp.any(p[:, None] == places[None, :], axis=0).astype(jnp.int32)
    kinds = level[None, :] == jnp.arange(NREC + 1, dtype=jnp.int32)[:, None]
    before = (places[:, None] < places[None, :]).astype(bf16)
    ahead = dot("ct,tu->cu", kinds.astype(bf16), before).astype(jnp.int32)
    bases = jnp.array([0, counts[2], counts[1], counts[0]], jnp.int32)
    position = jnp.sum(jnp.where(kinds, ahead + bases[:, None], 0), axis=0)
    chosen = position[None, :] == places[:, None]
    order = chosen.astype(bf16)
    token = jnp.sum(jnp.where(chosen, places[None, :], 0), axis=1)
    begin = jnp.sum(jnp.where(chosen, seq_start[None, :], 0), axis=1)
    frequency = jnp.exp(jnp.arange(HALF, dtype=f32) * (-2.0 * math.log(10000.0) / HEAD_DIM))
    angles = (token - begin).astype(f32)[:, None] * frequency[None, :]
    cos, sin = jnp.cos(angles), jnp.sin(angles)
    cos = jnp.concatenate([cos, cos], axis=1)
    sin = jnp.concatenate([-sin, sin], axis=1)
    rows2 = jnp.stack([token, begin]).astype(f32)
    cols2 = jnp.stack([token, begin], axis=1).astype(f32)
    tables = [(cos[:k], sin[:k], cols2[:k], rows2[:, :k]) for k in counts]

    hidden = dot("pt,td->pd", order, inputs)
    grads = dot("pt,td->pd", order, out_grad)

    kept, news, rows_in = [], [], hidden[: counts[0]]
    for r in range(NREC):
        new, saved = forward_step(rows_in, tables[r], weights, r)
        kept.append(saved)
        news.append(new)
        if r + 1 < NREC:
            rows_in = new[: counts[r + 1]]
    final = jnp.concatenate(
        [
            news[2].astype(bf16),
            news[1][counts[2] :].astype(bf16),
            news[0][counts[1] :].astype(bf16),
            hidden[counts[0] :].astype(bf16),
        ],
        axis=0,
    )
    result = dot("pt,pd->td", order, final).astype(bf16)

    grad_new = grads[: counts[2]]
    pairs, smalls = [], []
    for r in reversed(range(NREC)):
        grad_rows, step_pairs, step_small = backward_step(grad_new, kept[r], tables[r], weights, r)
        pairs.append(step_pairs)
        smalls.append(step_small)
        if r > 0:
            grad_new = jnp.concatenate([grad_rows, grads[counts[r] : counts[r - 1]]], axis=0)
    grad_final = jnp.concatenate([grad_rows.astype(bf16), grads[counts[0] :].astype(bf16)], axis=0)
    grad_inputs = dot("pt,pd->td", order, grad_final).astype(bf16)

    sums = []
    for i in range(5):
        left = jnp.concatenate([p[i][0] for p in pairs], axis=0)
        right = jnp.concatenate([p[i][1] for p in pairs], axis=0)
        sums.append(dot("kd,ke->de", left, right).astype(bf16))
    down, gate, up, out, qkv = sums
    down, gate, up = reduce_all(down), reduce_all(gate), reduce_all(up)
    first = reduce_all(jnp.concatenate([out, qkv], axis=1)).astype(f32)
    small = jnp.stack(
        [smalls[0][0] + smalls[1][0] + smalls[2][0], smalls[0][1] + smalls[1][1] + smalls[2][1]]
        + [s[2] for s in reversed(smalls)],
        axis=1,
    )
    small = lax.psum_scatter(small, "fsdp", scatter_dimension=0, tiled=True)
    small = lax.psum(small, "dp")
    return (
        result,
        grad_inputs,
        first[:, QW : 2 * QW],
        first[:, 2 * QW : 2 * QW + KW],
        first[:, 2 * QW + KW :],
        first[:, :QW],
        gate.astype(f32),
        up.astype(f32),
        down.astype(f32),
        small[:, 0],
        small[:, 1],
        small[:, 2:5],
    )


def solution(mesh):
    tok, row = P(("dp", "fsdp")), P("fsdp")
    in_specs = (tok,) + (row,) * 10 + (tok,) * 5
    out_specs = (tok, tok) + (row,) * 10
    return jax.shard_map(body, mesh=mesh, in_specs=in_specs, out_specs=out_specs, check_vma=False)
```

```python
import functools
import math

import jax
import jax.numpy as jnp
from jax import lax
from jax.experimental import pallas as pl
from jax.experimental.pallas import tpu as pltpu
from jax.sharding import PartitionSpec as P

HEADS = 15
KV_HEADS = 5
HEAD_DIM = 64
HALF = HEAD_DIM // 2
GROUP = HEADS // KV_HEADS
NREC = 3
ROWS = 256

norm_eps = 1e-05
masked_score = -1e30
highest = lax.Precision.HIGHEST
f32 = jnp.float32
bf16 = jnp.bfloat16


def dot(spec, left, right):
    return jnp.einsum(spec, left, right, preferred_element_type=f32)


def swap_halves(x):
    return jnp.concatenate([x[:, HALF:], x[:, :HALF]], axis=1)


def matmul(a, b, dims):
    return lax.dot_general(a, b, (dims, ((), ())), preferred_element_type=f32)


QW = HEADS * HEAD_DIM
KW = KV_HEADS * HEAD_DIM


def attend_fwd_kernel(qkv_ref, cos_ref, sin_ref, cols_ref, rows_ref, o_ref, q_ref, k_ref, v_ref, lse_ref, bias, stats):
    step = pl.program_id(0)
    rows = pl.ds(pl.multiple_of(step * ROWS, ROWS), ROWS)

    @pl.when(step == 0)
    def _():
        cos, sin = cos_ref[...], sin_ref[...]
        for g in range(KV_HEADS):
            raw = qkv_ref[:, QW + g * HEAD_DIM : QW + (g + 1) * HEAD_DIM]
            k_ref[g] = (raw * cos + swap_halves(raw) * sin).astype(bf16)
            v_ref[g] = qkv_ref[:, QW + KW + g * HEAD_DIM : QW + KW + (g + 1) * HEAD_DIM].astype(bf16)

    cols = cols_ref[rows, :]
    token, begin = cols[:, 0:1], cols[:, 1:2]
    key_token = rows_ref[0:1, :]
    bias[...] = jnp.where((key_token <= token) & (key_token >= begin), 0.0, masked_score)
    cos, sin = cos_ref[rows, :], sin_ref[rows, :]
    stats[...] = jnp.zeros_like(stats)
    for n in range(HEADS):
        g = n // GROUP
        raw = qkv_ref[rows, n * HEAD_DIM : (n + 1) * HEAD_DIM]
        q = ((raw * cos + swap_halves(raw) * sin).astype(bf16).astype(f32) * (1.0 / math.sqrt(HEAD_DIM))).astype(bf16)
        q_ref[n, rows, :] = q
        s = matmul(q, k_ref[g], ((1,), (1,))) + bias[...]
        m = jnp.max(s, axis=1, keepdims=True)
        p = jnp.exp(s - m)
        t = jnp.sum(p, axis=1, keepdims=True)
        p = (p * (1.0 / t)).astype(bf16)
        o_ref[rows, n * HEAD_DIM : (n + 1) * HEAD_DIM] = matmul(p, v_ref[g], ((1,), (0,))).astype(bf16)
        stats[:, n : n + 1] = m + jnp.log(t)
    lse_ref[...] = jnp.transpose(stats[...])[:16]


def attend_fwd(qkv, cos, sin, cols, rows):
    k = qkv.shape[0]
    whole = lambda *shape: pl.BlockSpec(shape, lambda i: (0,) * len(shape))
    return pl.pallas_call(
        attend_fwd_kernel,
        grid=(k // ROWS,),
        out_shape=(
            jax.ShapeDtypeStruct((k, QW), bf16),
            jax.ShapeDtypeStruct((HEADS, k, HEAD_DIM), bf16),
            jax.ShapeDtypeStruct((KV_HEADS, k, HEAD_DIM), bf16),
            jax.ShapeDtypeStruct((KV_HEADS, k, HEAD_DIM), bf16),
            jax.ShapeDtypeStruct((16, k), f32),
        ),
        in_specs=[
            whole(k, QW + 2 * KW),
            whole(k, HEAD_DIM),
            whole(k, HEAD_DIM),
            whole(k, 2),
            whole(2, k),
        ],
        out_specs=(
            whole(k, QW),
            whole(HEADS, k, HEAD_DIM),
            whole(KV_HEADS, k, HEAD_DIM),
            whole(KV_HEADS, k, HEAD_DIM),
            pl.BlockSpec((16, ROWS), lambda i: (0, i)),
        ),
        scratch_shapes=[pltpu.VMEM((ROWS, k), f32), pltpu.VMEM((ROWS, 128), f32)],
        compiler_params=pltpu.CompilerParams(vmem_limit_bytes=56 << 20),
        name="attend_fwd",
    )(qkv, cos, sin, cols, rows)


def attend_bwd_kernel(
    q_ref, k_ref, v_ref, lse_ref, do_ref, cos_ref, sin_ref, cols_ref, rows_ref, out_ref, bias, dk, dv, kt
):
    step = pl.program_id(0)
    start = pl.multiple_of(step * ROWS, ROWS)
    rows = pl.ds(start, ROWS)

    @pl.when(step == 0)
    def _():
        dk[...] = jnp.zeros_like(dk)
        dv[...] = jnp.zeros_like(dv)
        for g in range(KV_HEADS):
            kt[g] = jnp.transpose(k_ref[g].astype(f32)).astype(bf16)

    key_token = cols_ref[:, 0:1]
    token, begin = rows_ref[0:1, pl.ds(start, ROWS)], rows_ref[1:2, pl.ds(start, ROWS)]
    bias[...] = jnp.where((key_token <= token) & (key_token >= begin), 0.0, masked_score)
    cos, sin = cos_ref[rows, :], sin_ref[rows, :]
    for n in range(HEADS):
        g = n // GROUP
        q = q_ref[n, rows, :]
        do = do_ref[rows, n * HEAD_DIM : (n + 1) * HEAD_DIM]
        s = matmul(k_ref[g], q, ((1,), (1,))) + bias[...]
        p = jnp.exp(s - lse_ref[n : n + 1, :])
        dp = matmul(v_ref[g], do, ((1,), (1,)))
        dv[g] += matmul(p.astype(bf16), do, ((1,), (0,)))
        pd = p * dp
        ds = (pd - p * jnp.sum(pd, axis=0, keepdims=True)).astype(bf16)
        dk[g] += matmul(ds, q, ((1,), (0,)))
        dq = jnp.transpose(matmul(kt[g], ds, ((1,), (0,)))) * (1.0 / math.sqrt(HEAD_DIM))
        out_ref[rows, n * HEAD_DIM : (n + 1) * HEAD_DIM] = (dq * cos - swap_halves(dq) * sin).astype(bf16)

    @pl.when(step == pl.num_programs(0) - 1)
    def _():
        cos, sin = cos_ref[...], sin_ref[...]
        for g in range(KV_HEADS):
            grad = dk[g]
            out_ref[:, QW + g * HEAD_DIM : QW + (g + 1) * HEAD_DIM] = (
                grad * cos - swap_halves(grad) * sin
            ).astype(bf16)
            out_ref[:, QW + KW + g * HEAD_DIM : QW + KW + (g + 1) * HEAD_DIM] = dv[g].astype(bf16)


def attend_bwd(q, k, v, lse, grad, cos, sin, cols, rows):
    count = grad.shape[0]
    whole = lambda *shape: pl.BlockSpec(shape, lambda i: (0,) * len(shape))
    return pl.pallas_call(
        attend_bwd_kernel,
        grid=(count // ROWS,),
        out_shape=jax.ShapeDtypeStruct((count, QW + 2 * KW), bf16),
        in_specs=[
            whole(HEADS, count, HEAD_DIM),
            whole(KV_HEADS, count, HEAD_DIM),
            whole(KV_HEADS, count, HEAD_DIM),
            pl.BlockSpec((16, ROWS), lambda i: (0, i)),
            whole(count, QW),
            whole(count, HEAD_DIM),
            whole(count, HEAD_DIM),
            whole(count, 2),
            whole(2, count),
        ],
        out_specs=whole(count, QW + 2 * KW),
        scratch_shapes=[
            pltpu.VMEM((count, ROWS), f32),
            pltpu.VMEM((KV_HEADS, count, HEAD_DIM), f32),
            pltpu.VMEM((KV_HEADS, count, HEAD_DIM), f32),
            pltpu.VMEM((KV_HEADS, HEAD_DIM, count), bf16),
        ],
        compiler_params=pltpu.CompilerParams(vmem_limit_bytes=56 << 20),
        name="attend_bwd",
    )(q, k, v, lse, grad, cos, sin, cols, rows)


def inverse_rms(values):
    return lax.rsqrt(jnp.mean(values * values, axis=-1, keepdims=True) + norm_eps)


def norm_back(values, gain, grad):
    scale = inverse_rms(values)
    unit = values * scale
    grad_unit = grad * gain
    grad_values = (grad_unit - unit * jnp.mean(grad_unit * unit, axis=-1, keepdims=True)) * scale
    return grad_values, jnp.sum(grad * unit, axis=0)


def forward_step(rows_in, tables, weights, section):
    wqkv, wo, wg, wu, wd, gain_attn, gain_ffn, router = weights
    normed = (rows_in * inverse_rms(rows_in) * gain_attn).astype(bf16)
    qkv = dot("kd,de->ke", normed, wqkv)
    mixed, q, k, v, lse = attend_fwd(qkv, *tables)
    attn = dot("ke,ed->kd", mixed, wo)
    middle = rows_in + attn
    inner = (middle * inverse_rms(middle) * gain_ffn).astype(bf16)
    gate = dot("kd,df->kf", inner, wg)
    up = dot("kd,df->kf", inner, wu)
    activated = (gate * jax.nn.sigmoid(gate) * up).astype(bf16)
    ffn = dot("kf,fd->kd", activated, wd)
    gate_c = jax.nn.sigmoid(jnp.sum(rows_in * router[:, section][None, :], axis=1, keepdims=True))
    branches = attn + ffn
    out = rows_in + gate_c * branches
    kept = (rows_in, normed, q, k, v, lse, mixed, middle, inner, gate.astype(bf16), up.astype(bf16), activated, gate_c, branches)
    return out, kept


def backward_step(grad_new, kept, tables, weights, section):
    wqkv, wo, wg, wu, wd, gain_attn, gain_ffn, router = weights
    rows_in, normed, q, k, v, lse, mixed, middle, inner, gate, up, activated, gate_c, branches = kept
    gate, up = gate.astype(f32), up.astype(f32)
    dz = jnp.sum(grad_new * branches, axis=1, keepdims=True) * gate_c * (1.0 - gate_c)
    router_grad = jnp.sum(rows_in * dz, axis=0)
    grad_rows = grad_new + dz * router[:, section][None, :]
    grad_branch = gate_c * grad_new
    grad_ffn = grad_branch.astype(bf16)
    grad_act = dot("kd,fd->kf", grad_ffn, wd)
    sig = jax.nn.sigmoid(gate)
    grad_gate = (grad_act * up * (sig + gate * sig * (1.0 - sig))).astype(bf16)
    grad_up = (grad_act * (gate * sig)).astype(bf16)
    grad_inner = dot("kf,df->kd", grad_gate, wg) + dot("kf,df->kd", grad_up, wu)
    grad_middle, gain_ffn_grad = norm_back(middle, gain_ffn, grad_inner)
    grad_attn = (grad_branch + grad_middle).astype(bf16)
    grad_mixed = dot("kd,ed->ke", grad_attn, wo).astype(bf16)
    grad_qkv = attend_bwd(q, k, v, lse, grad_mixed, *tables)
    grad_normed = dot("ke,de->kd", grad_qkv, wqkv)
    grad_norm_rows, gain_attn_grad = norm_back(rows_in, gain_attn, grad_normed)
    grad_rows = grad_rows + grad_middle + grad_norm_rows
    pairs = ((activated, grad_ffn), (inner, grad_gate), (inner, grad_up), (mixed, grad_attn), (normed, grad_qkv))
    return grad_rows, pairs, (gain_attn_grad, gain_ffn_grad, router_grad)


MESH = pl.DeviceIdType.MESH
GATHER_ORDER = (0, 1, 2, 3)


def place():
    d, z = lax.axis_index("dp"), lax.axis_index("fsdp")
    c, x, y = lax.rem(d, 2), lax.rem(lax.div(d, 2), 2), lax.div(d, 4)
    ids = dict(
        core={"dp": d + 1 - 2 * c},
        x={"dp": d + 2 - 4 * x},
        y={"dp": d + 4 - 8 * y},
        up={"fsdp": z + 1},
        down={"fsdp": z - 1},
    )
    return z, c, x, y, ids


def greet(z, ids):
    barrier = pltpu.get_barrier_semaphore()
    for name in ("core", "x", "y"):
        pl.semaphore_signal(barrier, inc=1, device_id=ids[name], device_id_type=MESH)

    @pl.when(z < 3)
    def _():
        pl.semaphore_signal(barrier, inc=1, device_id=ids["up"], device_id_type=MESH)

    @pl.when(z > 0)
    def _():
        pl.semaphore_signal(barrier, inc=1, device_id=ids["down"], device_id_type=MESH)

    pl.semaphore_wait(barrier, 5 - lax.div(z, 3) - lax.div(3 - z, 3))


def remote(src, dst, send, recv, target):
    return pltpu.make_async_remote_copy(
        src_ref=src, dst_ref=dst, send_sem=send, recv_sem=recv, device_id=target, device_id_type=MESH
    )


def piece(ref, a, lead, p, parts=4):
    if a < 3:
        width = ref.shape[-1] // parts
        return ref.at[(*lead, slice(None), pl.ds(pl.multiple_of(p * width, 128), width))]
    height = ref.shape[-2] // parts
    return ref.at[(*lead, pl.ds(pl.multiple_of(p * height, 16), height), slice(None))]


def pieces_of(a, x, y):
    f, s, wf, ws = (y, x, 2, 1) if a < 2 else (x, y, 2, 1)
    own = 2 * f + s
    nx = 2 * f + 1 - s if a < 2 else 2 * (1 - f) + s
    ny = 2 * (1 - f) + s if a < 2 else 2 * f + 1 - s
    return own, nx, ny, 2 * (1 - f) + 1 - s


def plane_stage(stage, refs, a, slot, lead, where, send, recv):
    z, c, x, y, ids = where
    own, nx, ny, far = pieces_of(a, x, y)
    first = [(own, "x", 0), (own, "y", 1), (own, "core", 3)]
    second = [(nx, "core", 4), (ny, "core", 5), (ny, "x", 2) if a < 2 else (nx, "y", 2)]
    third = [(far, "core", 6)]

    def copy(p, name, kind):
        part = piece(refs[a], a, lead, p)
        return remote(part, part, send.at[kind, a, slot], recv.at[kind, a, slot], ids[name])

    def arrived(p, kind):
        part = piece(refs[a], a, lead, p)
        remote(part, part, send.at[kind, a, slot], recv.at[kind, a, slot], ids["core"]).wait_recv()

    if stage == 1:
        for item in first:
            copy(*item).start()
    elif stage == 2:
        arrived(nx, 0)
        copy(*second[0]).start()
        arrived(ny, 1)
        copy(*second[1]).start()
        copy(*second[2]).start()
    elif stage == 3:
        arrived(far, 2)
        copy(*third[0]).start()
    else:
        other = (*lead[:-1], 1 - c)
        for p, kind in ((own, 3), (nx, 4), (ny, 5), (far, 6)):
            part = piece(refs[a], a, other, p)
            remote(part, part, send.at[kind, a, slot], recv.at[kind, a, slot], ids["core"]).wait_recv()
        for item in first + second + third:
            copy(*item).wait_send()


def gather_kernel(s0, s1, s2, s3, small, o0, o1, o2, o3, small_out, send, recv, zsend, zrecv, local):
    where = place()
    z, c, x, y, ids = where
    shards, outs = (s0, s1, s2, s3), (o0, o1, o2, o3)
    greet(z, ids)

    def along(a, origin, way):
        if a == 4:
            dst = small_out.at[origin]
            src = dst
        else:
            dst = src = piece(outs[a], a, (origin, c), pieces_of(a, x, y)[0])
        way_index = 0 if way == "up" else 1
        return src, dst, zsend.at[way_index, a, origin], zrecv.at[a, origin], ids[way]

    def own_copy(a, way):
        src, dst, ss, rs, target = along(a, z, way)
        src = small if a == 4 else piece(shards[a], a, (c,), pieces_of(a, x, y)[0])
        return remote(src, dst, ss, rs, target)

    kinds = (4,) + GATHER_ORDER

    @pl.when(z < 3)
    def _():
        for a in kinds:
            own_copy(a, "up").start()

    @pl.when(z > 0)
    def _():
        for a in kinds:
            own_copy(a, "down").start()

    def own_local(a):
        if a == 4:
            return pltpu.make_async_copy(small, small_out.at[z], local.at[a])
        return pltpu.make_async_copy(shards[a], outs[a].at[z], local.at[a])

    for a in kinds:
        own_local(a).start()

    def foreign(step, a, stage):
        for way, origin, there, more in (
            ("up", z - step, z >= step, z < 3),
            ("down", z + step, z <= 3 - step, z > 0),
        ):

            @pl.when(there)
            def _():
                if stage == 1:
                    remote(*along(a, origin, way)).wait_recv()

                    @pl.when(more)
                    def _():
                        remote(*along(a, origin, way)).start()

                if a < 4:
                    plane_stage(stage, outs, a, origin, (origin, c), where, send, recv)
                if stage == 4:

                    @pl.when(more)
                    def _():
                        remote(*along(a, origin, way)).wait_send()

    for step in (1, 2, 3):
        foreign(step, 4, 1)
    events = [(step, a) for step in (1, 2, 3) for a in GATHER_ORDER]
    for k in range(len(events) + 4):
        if k < len(events):
            foreign(*events[k], 1)
        if 2 <= k < len(events) + 2:
            foreign(*events[k - 2], 2)
        if 4 <= k:
            foreign(*events[k - 4], 3)
    for a in kinds:
        for step in (1, 2, 3):
            foreign(step, a, 4)

    @pl.when(z < 3)
    def _():
        for a in kinds:
            own_copy(a, "up").wait_send()

    @pl.when(z > 0)
    def _():
        for a in kinds:
            own_copy(a, "down").wait_send()

    for a in kinds:
        own_local(a).wait()


def gather_weights(shards, small):
    dma = pltpu.SemaphoreType.DMA
    vmem, hbm = pl.BlockSpec(memory_space=pltpu.VMEM), pl.BlockSpec(memory_space=pl.ANY)
    halves = [s.reshape(2, s.shape[0] // 2, s.shape[1]) for s in shards]
    out = pl.pallas_call(
        gather_kernel,
        out_shape=tuple(jax.ShapeDtypeStruct((4, *s.shape), s.dtype) for s in halves + [small]),
        in_specs=[vmem] * 5,
        out_specs=[hbm] * 5,
        scratch_shapes=[dma((7, 4, 4)), dma((7, 4, 4)), dma((2, 5, 4)), dma((5, 4)), dma((5,))],
        compiler_params=pltpu.CompilerParams(collective_id=0, has_side_effects=True, vmem_limit_bytes=32 << 20),
        name="gather_weights",
    )(*halves, small)
    return [o.reshape(-1, o.shape[-1]) for o in out[:4]], out[4]


TARGETS = (3, 0, 2, 1)


def add_into(dst, dlead, drow, dcol, src, slead, rows, cols):
    wide = cols % 640 == 0
    count = cols // 640 if wide else rows // 80

    def one(i):
        if wide:
            shift = pl.multiple_of(i * 640, 128)
            at_src = (*slead, slice(None), pl.ds(shift, 640))
            at_dst = (*dlead, slice(None), pl.ds(pl.multiple_of(dcol + shift, 128), 640))
        else:
            shift = pl.multiple_of(i * 80, 16)
            at_src = (*slead, pl.ds(shift, 80), slice(None))
            at_dst = (*dlead, pl.ds(pl.multiple_of(drow + shift, 16), 80), slice(None))
        dst[at_dst] = (dst[at_dst].astype(f32) + src[at_src].astype(f32)).astype(dst.dtype)

    if count == 1:
        one(0)
    else:

        @pl.loop(0, count)
        def _(i):
            one(i)


def reduce_kernel(
    g0, g1, g2, g3, small, o0, o1, o2, o3, small_out,
    a0, a1, a2, a3, c0, c1, c2, c3, p0, p1, p2, p3, q0, q1, q2, q3, u0, u1, u2, u3, d0, d1, d2, d3,
    small_in, small_out_buf, csend, crecv, psend, precv, zsend, zrecv, send, recv, loads, ssend, srecv,
):
    where = place()
    z, c, x, y, ids = where
    full, outs, acc, cbuf = (g0, g1, g2, g3), (o0, o1, o2, o3), (a0, a1, a2, a3), (c0, c1, c2, c3)
    first, second = (p0, p1, p2, p3), (q0, q1, q2, q3)
    up, down = (u0, u1, u2, u3), (d0, d1, d2, d3)
    greet(z, ids)

    def load(a, t):
        return pltpu.make_async_copy(full[a].at[t, c], acc[a].at[t], loads.at[a, t])

    def core_copy(a, t):
        return remote(full[a].at[t, 1 - c], cbuf[a].at[t], csend.at[a, t], crecv.at[a, t], ids["core"])

    def coords(a):
        return (y, x, "y", "x") if a < 2 else (x, y, "x", "y")

    def first_copy(a, t):
        f, s, nf, ns = coords(a)
        return remote(piece(acc[a], a, (t,), 1 - f, 2), first[a].at[t], psend.at[0, a, t], precv.at[0, a, t], ids[nf])

    def second_copy(a, t):
        f, s, nf, ns = coords(a)
        return remote(
            piece(acc[a], a, (t,), 2 * f + 1 - s), second[a].at[t], psend.at[1, a, t], precv.at[1, a, t], ids[ns]
        )

    def own_piece(a, t):
        f, s, nf, ns = coords(a)
        return piece(acc[a], a, (t,), 2 * f + s)

    def up_copy(a, t):
        return remote(own_piece(a, t), up[a].at[t], zsend.at[0, a, t], zrecv.at[0, a, t], ids["up"])

    def down_copy(a, t):
        return remote(own_piece(a, t), down[a].at[t], zsend.at[1, a, t], zrecv.at[1, a, t], ids["down"])

    def add_piece(a, t, src, index, parts):
        rows, cols = src.shape[-2:]
        offset = index * (acc[a].shape[-1] // parts if a < 3 else acc[a].shape[-2] // parts)
        add_into(acc[a], (t,), 0 if a < 3 else offset, offset if a < 3 else 0, src, (t,), rows, cols)

    def stage2(t):
        for a in range(4):
            load(a, t).wait()
            core_copy(a, t).wait_recv()
            add_piece(a, t, cbuf[a], 0, 1)
            first_copy(a, t).start()

    def stage3(t):
        for a in range(4):
            first_copy(a, t).wait_recv()
            add_piece(a, t, first[a], coords(a)[0], 2)
            second_copy(a, t).start()

    def own_index(a):
        f, s, nf, ns = coords(a)
        return 2 * f + s

    def stage4(t):
        for a in range(4):
            second_copy(a, t).wait_recv()
            add_piece(a, t, second[a], own_index(a), 4)

            if t > 0:

                @pl.when(z == 0)
                def _():
                    up_copy(a, t).start()

            if t < 3:

                @pl.when(z == 3)
                def _():
                    down_copy(a, t).start()

    def stage5(t):
        for a in range(4):
            if t > 0:

                @pl.when((z > 0) & (z <= t))
                def _():
                    up_copy(a, t).wait_recv()
                    add_piece(a, t, up[a], own_index(a), 4)

                @pl.when((z > 0) & (z < t))
                def _():
                    up_copy(a, t).start()

            if t < 3:

                @pl.when((z < 3) & (z >= t))
                def _():
                    down_copy(a, t).wait_recv()
                    add_piece(a, t, down[a], own_index(a), 4)

                @pl.when((z < 3) & (z > t))
                def _():
                    down_copy(a, t).start()

    def small_copy(k, name):
        return remote(small_out_buf.at[k], small_in.at[k], ssend.at[k], srecv.at[k], ids[name])

    for t in TARGETS:
        for a in range(4):
            core_copy(a, t).start()
            load(a, t).start()
    total = small[...]
    for k, name in enumerate(("core", "x", "y")):
        small_out_buf[k] = total
        small_copy(k, name).start()
        small_copy(k, name).wait_recv()
        total = total + small_in[k]
    small_out[...] = total

    n = len(TARGETS)
    for k in range(n + 3):
        if k < n:
            stage2(TARGETS[k])
        if 1 <= k < n + 1:
            stage3(TARGETS[k - 1])
        if 2 <= k < n + 2:
            stage4(TARGETS[k - 2])
        if 3 <= k:
            stage5(TARGETS[k - 3])

    small_out_buf[3] = small_out[...]
    small_out_buf[4] = small_out[...]

    @pl.when(z > 0)
    def _():
        small_copy(3, "up").wait_recv()
        small_out_buf[3] = small_out_buf[3] + small_in[3]

    @pl.when(z < 3)
    def _():
        small_copy(3, "up").start()
        small_copy(4, "down").wait_recv()
        small_out_buf[4] = small_out_buf[4] + small_in[4]

    @pl.when(z > 0)
    def _():
        small_copy(4, "down").start()

    small_out[...] = small_out_buf[3] + small_out_buf[4] - small_out[...]

    for a in range(4):
        src = own_piece(a, z)
        dst = piece(outs[a], a, (c,), own_index(a))
        dst[...] = src[...]
        plane_stage(1, outs, a, 0, (c,), where, send, recv)
    for stage in (2, 3, 4):
        for a in range(4):
            plane_stage(stage, outs, a, 0, (c,), where, send, recv)

    for k, name in enumerate(("core", "x", "y")):
        small_copy(k, name).wait_send()

    @pl.when(z < 3)
    def _():
        small_copy(3, "up").wait_send()

    @pl.when(z > 0)
    def _():
        small_copy(4, "down").wait_send()

    for t in range(4):
        for a in range(4):
            core_copy(a, t).wait_send()
            first_copy(a, t).wait_send()
            second_copy(a, t).wait_send()
            if t > 0:

                @pl.when(z < t)
                def _():
                    up_copy(a, t).wait_send()

            if t < 3:

                @pl.when(z > t)
                def _():
                    down_copy(a, t).wait_send()


def reduce_grads(grads, small):
    dma = pltpu.SemaphoreType.DMA
    vmem, hbm = pl.BlockSpec(memory_space=pltpu.VMEM), pl.BlockSpec(memory_space=pl.ANY)
    full = [g.reshape(4, 2, g.shape[0] // 8, g.shape[1]) for g in grads]

    def buffers(parts):
        shapes = []
        for a, g in enumerate(full):
            rows, cols = g.shape[2:]
            shapes.append((4, rows, cols // parts) if a < 3 else (4, rows // parts, cols))
        return [pltpu.VMEM(s, bf16) for s in shapes]

    out = pl.pallas_call(
        reduce_kernel,
        out_shape=tuple(jax.ShapeDtypeStruct(g.shape[1:], bf16) for g in full)
        + (jax.ShapeDtypeStruct(small.shape, f32),),
        in_specs=[hbm] * 4 + [vmem],
        out_specs=[vmem] * 5,
        scratch_shapes=buffers(1) + buffers(1) + buffers(2) + buffers(4) + buffers(4) + buffers(4)
        + [pltpu.VMEM((5, *small.shape), f32)] * 2
        + [dma((4, 4)), dma((4, 4)), dma((2, 4, 4)), dma((2, 4, 4)), dma((2, 4, 4)), dma((2, 4, 4))]
        + [dma((7, 4, 1)), dma((7, 4, 1)), dma((4, 4)), dma((5,)), dma((5,))],
        compiler_params=pltpu.CompilerParams(collective_id=1, has_side_effects=True, vmem_limit_bytes=60 << 20),
        name="reduce_grads",
    )(*full, small)
    return [o.reshape(-1, o.shape[-1]) for o in out[:4]], out[4]


def gather_all(shard):
    if shard.shape[0] % lax.axis_size("dp"):
        return lax.all_gather(shard, "fsdp", axis=0, tiled=True)
    rows = shard.shape[0] // lax.axis_size("dp")
    part = lax.dynamic_slice_in_dim(shard, lax.axis_index("dp") * rows, rows, 0)
    return lax.all_gather(part, ("fsdp", "dp"), axis=0, tiled=True)


def reduce_all(total):
    chunks = lax.axis_size("dp") * lax.axis_size("fsdp")
    if total.shape[0] % chunks:
        part = lax.psum_scatter(total, "fsdp", scatter_dimension=0, tiled=True)
        return lax.psum(part, "dp")
    rows = total.shape[0] // chunks
    padded = jnp.pad(total.reshape(chunks, rows, -1), ((0, 0), (0, -rows % 16), (0, 0)))
    part = lax.psum_scatter(padded.reshape(-1, total.shape[1]), ("fsdp", "dp"), scatter_dimension=0, tiled=True)[:rows]
    return lax.all_gather(part, "dp", axis=0, tiled=True)


def body(
    inputs, w_query, w_key, w_value, w_out, w_gate, w_up, w_down, gain_attn, gain_ffn, w_router,
    seq_start, pick_first, pick_second, pick_third, out_grad,
):
    picks = (pick_first, pick_second, pick_third)
    counts = tuple(p.shape[0] for p in picks)
    tokens = inputs.shape[0]

    by_kernel = lax.axis_size("dp") == 8 and lax.axis_size("fsdp") == 4
    owned = gain_attn.shape[0]
    first = jnp.concatenate([w_out, w_query, w_key, w_value], axis=1)
    small = jnp.concatenate([gain_attn[None], gain_ffn[None], w_router.T], axis=0)
    if by_kernel:
        small = jnp.pad(small, ((0, 16 - small.shape[0]), (0, -owned % 128)))
        (first, wg, wu, wd), small = gather_weights([first, w_gate, w_up, w_down], small)
        small = small[:, :, :owned].transpose(1, 0, 2).reshape(16, -1).astype(f32)
    else:
        first, wg, wu, wd = gather_all(first), gather_all(w_gate), gather_all(w_up), gather_all(w_down)
        small = lax.all_gather(small, "fsdp", axis=1, tiled=True).astype(f32)
    wo, wqkv = first[:, :QW], first[:, QW:]
    weights = (wqkv, wo, wg, wu, wd, small[0], small[1], small[2 : 2 + NREC].T)

    places = jnp.arange(tokens, dtype=jnp.int32)
    level = jnp.full((tokens,), NREC, jnp.int32)
    for p in picks:
        level = level - jnp.any(p[:, None] == places[None, :], axis=0).astype(jnp.int32)
    kinds = level[None, :] == jnp.arange(NREC + 1, dtype=jnp.int32)[:, None]
    before = (places[:, None] < places[None, :]).astype(bf16)
    ahead = dot("ct,tu->cu", kinds.astype(bf16), before).astype(jnp.int32)
    bases = jnp.array([0, counts[2], counts[1], counts[0]], jnp.int32)
    position = jnp.sum(jnp.where(kinds, ahead + bases[:, None], 0), axis=0)
    chosen = position[None, :] == places[:, None]
    order = chosen.astype(bf16)
    token = jnp.sum(jnp.where(chosen, places[None, :], 0), axis=1)
    begin = jnp.sum(jnp.where(chosen, seq_start[None, :], 0), axis=1)
    frequency = jnp.exp(jnp.arange(HALF, dtype=f32) * (-2.0 * math.log(10000.0) / HEAD_DIM))
    angles = (token - begin).astype(f32)[:, None] * frequency[None, :]
    cos, sin = jnp.cos(angles), jnp.sin(angles)
    cos = jnp.concatenate([cos, cos], axis=1)
    sin = jnp.concatenate([-sin, sin], axis=1)
    rows2 = jnp.stack([token, begin]).astype(f32)
    cols2 = jnp.stack([token, begin], axis=1).astype(f32)
    tables = [(cos[:k], sin[:k], cols2[:k], rows2[:, :k]) for k in counts]

    hidden = dot("pt,td->pd", order, inputs)
    grads = dot("pt,td->pd", order, out_grad)

    kept, news, rows_in = [], [], hidden[: counts[0]]
    for r in range(NREC):
        new, saved = forward_step(rows_in, tables[r], weights, r)
        kept.append(saved)
        news.append(new)
        if r + 1 < NREC:
            rows_in = new[: counts[r + 1]]
    final = jnp.concatenate(
        [
            news[2].astype(bf16),
            news[1][counts[2] :].astype(bf16),
            news[0][counts[1] :].astype(bf16),
            hidden[counts[0] :].astype(bf16),
        ],
        axis=0,
    )
    result = dot("pt,pd->td", order, final).astype(bf16)

    grad_new = grads[: counts[2]]
    pairs, smalls = [], []
    for r in reversed(range(NREC)):
        grad_rows, step_pairs, step_small = backward_step(grad_new, kept[r], tables[r], weights, r)
        pairs.append(step_pairs)
        smalls.append(step_small)
        if r > 0:
            grad_new = jnp.concatenate([grad_rows, grads[counts[r] : counts[r - 1]]], axis=0)
    grad_final = jnp.concatenate([grad_rows.astype(bf16), grads[counts[0] :].astype(bf16)], axis=0)
    grad_inputs = dot("pt,pd->td", order, grad_final).astype(bf16)

    sums = []
    for i in range(5):
        left = jnp.concatenate([p[i][0] for p in pairs], axis=0)
        right = jnp.concatenate([p[i][1] for p in pairs], axis=0)
        sums.append(dot("kd,ke->de", left, right).astype(bf16))
    down, gate, up, out, qkv = sums
    first = jnp.concatenate([out, qkv], axis=1)
    small = jnp.stack(
        [smalls[0][0] + smalls[1][0] + smalls[2][0], smalls[0][1] + smalls[1][1] + smalls[2][1]]
        + [s[2] for s in reversed(smalls)]
    )
    if by_kernel:
        small = jnp.pad(small, ((0, 8 - small.shape[0]), (0, -small.shape[1] % 128)))
        (first, gate, up, down), small = reduce_grads([first, gate, up, down], small)
        small = lax.dynamic_slice_in_dim(small, lax.axis_index("fsdp") * owned, owned, 1)
    else:
        first, gate, up, down = reduce_all(first), reduce_all(gate), reduce_all(up), reduce_all(down)
        small = lax.psum_scatter(small, "fsdp", scatter_dimension=1, tiled=True)
        small = lax.psum(small, "dp")
    first = first.astype(f32)
    return (
        result,
        grad_inputs,
        first[:, QW : 2 * QW],
        first[:, 2 * QW : 2 * QW + KW],
        first[:, 2 * QW + KW :],
        first[:, :QW],
        gate.astype(f32),
        up.astype(f32),
        down.astype(f32),
        small[0],
        small[1],
        small[2 : 2 + NREC].T,
    )


def solution(mesh):
    tok, row = P(("dp", "fsdp")), P("fsdp")
    in_specs = (tok,) + (row,) * 10 + (tok,) * 5
    out_specs = (tok, tok) + (row,) * 10
    return jax.shard_map(body, mesh=mesh, in_specs=in_specs, out_specs=out_specs, check_vma=False)
```

```python
import functools
import math

import jax
import jax.numpy as jnp
from jax import lax
from jax.experimental import pallas as pl
from jax.experimental.pallas import tpu as pltpu
from jax.sharding import PartitionSpec as P

HEADS = 15
KV_HEADS = 5
HEAD_DIM = 64
HALF = HEAD_DIM // 2
GROUP = HEADS // KV_HEADS
NREC = 3
ROWS = 256

norm_eps = 1e-05
masked_score = -1e30
highest = lax.Precision.HIGHEST
f32 = jnp.float32
bf16 = jnp.bfloat16


def dot(spec, left, right):
    return jnp.einsum(spec, left, right, preferred_element_type=f32)


def swap_halves(x):
    return jnp.concatenate([x[:, HALF:], x[:, :HALF]], axis=1)


def matmul(a, b, dims):
    return lax.dot_general(a, b, (dims, ((), ())), preferred_element_type=f32)


QW = HEADS * HEAD_DIM
KW = KV_HEADS * HEAD_DIM


def attend_fwd_kernel(
    qkv_ref, cos_ref, sin_ref, cols_ref, rows_ref, o_ref, q_ref, k_ref, v_ref, lse_ref, bias, vt
):
    step = pl.program_id(0)
    start = pl.multiple_of(step * ROWS, ROWS)
    rows = pl.ds(start, ROWS)

    def turned(at, column, cos, sin):
        raw = qkv_ref[at, column : column + 128]
        lane = lax.broadcasted_iota(jnp.int32, raw.shape, 1)
        swapped = jnp.where(lax.rem(lane, HEAD_DIM) < HALF, pltpu.roll(raw, 128 - HALF, 1), pltpu.roll(raw, HALF, 1))
        return raw * cos + swapped * sin

    @pl.when(step == 0)
    def _():
        everything = slice(None)
        cos, sin = cos_ref[...], sin_ref[...]
        for column in range(QW // 128 * 128, QW + KW, 128):
            keys = turned(everything, column, cos, sin).astype(bf16)
            for part in range(2):
                g = (column + part * HEAD_DIM - QW) // HEAD_DIM
                if 0 <= g < KV_HEADS:
                    k_ref[g] = keys[:, part * HEAD_DIM : (part + 1) * HEAD_DIM]
        for g in range(KV_HEADS):
            value = qkv_ref[:, QW + KW + g * HEAD_DIM : QW + KW + (g + 1) * HEAD_DIM]
            v_ref[g] = value.astype(bf16)
            vt[g] = jnp.transpose(value).astype(bf16)

    key_token = cols_ref[:, 0:1]
    token, begin = rows_ref[0:1, pl.ds(start, ROWS)], rows_ref[1:2, pl.ds(start, ROWS)]
    bias[...] = jnp.where((key_token <= token) & (key_token >= begin), 0.0, masked_score)
    scale = 1.0 / math.sqrt(HEAD_DIM)
    cos, sin = cos_ref[rows, :] * scale, sin_ref[rows, :] * scale
    for first in range(0, HEADS, 2):
        pair = turned(rows, first * HEAD_DIM, cos, sin).astype(bf16)
        outs = []
        for n in range(first, min(first + 2, HEADS)):
            g = n // GROUP
            q = pair[:, (n - first) * HEAD_DIM : (n - first + 1) * HEAD_DIM]
            q_ref[n, rows, :] = q
            s = matmul(k_ref[g], q, ((1,), (1,))) + bias[...]
            m = jnp.max(s, axis=0, keepdims=True)
            p = jnp.exp(s - m)
            t = jnp.sum(p, axis=0, keepdims=True)
            p = (p * (1.0 / t)).astype(bf16)
            outs.append(matmul(vt[g], p, ((1,), (0,))))
            lse_ref[n : n + 1, :] = m + jnp.log(t)
        width = HEAD_DIM * len(outs)
        o_ref[rows, first * HEAD_DIM : first * HEAD_DIM + width] = jnp.transpose(jnp.concatenate(outs, axis=0)).astype(
            bf16
        )


def attend_fwd(qkv, cos, sin, cos_t, sin_t, cols, rows):
    k = qkv.shape[0]
    whole = lambda *shape: pl.BlockSpec(shape, lambda i: (0,) * len(shape))
    return pl.pallas_call(
        attend_fwd_kernel,
        grid=(k // ROWS,),
        out_shape=(
            jax.ShapeDtypeStruct((k, QW), bf16),
            jax.ShapeDtypeStruct((HEADS, k, HEAD_DIM), bf16),
            jax.ShapeDtypeStruct((KV_HEADS, k, HEAD_DIM), bf16),
            jax.ShapeDtypeStruct((KV_HEADS, k, HEAD_DIM), bf16),
            jax.ShapeDtypeStruct((16, k), f32),
        ),
        in_specs=[
            whole(k, QW + 2 * KW),
            whole(k, 2 * HEAD_DIM),
            whole(k, 2 * HEAD_DIM),
            whole(k, 2),
            whole(2, k),
        ],
        out_specs=(
            whole(k, QW),
            whole(HEADS, k, HEAD_DIM),
            whole(KV_HEADS, k, HEAD_DIM),
            whole(KV_HEADS, k, HEAD_DIM),
            pl.BlockSpec((16, ROWS), lambda i: (0, i)),
        ),
        scratch_shapes=[pltpu.VMEM((k, ROWS), f32), pltpu.VMEM((KV_HEADS, HEAD_DIM, k), bf16)],
        compiler_params=pltpu.CompilerParams(vmem_limit_bytes=56 << 20),
        name="attend_fwd",
    )(qkv, cos, sin, cols, rows)


def attend_bwd_kernel(
    q_ref, k_ref, v_ref, lse_ref, do_ref, cos_ref, sin_ref, cos_t_ref, sin_t_ref, cols_ref, rows_ref, out_ref,
    bias, dk, dv, kt,
):
    step = pl.program_id(0)
    start = pl.multiple_of(step * ROWS, ROWS)
    rows = pl.ds(start, ROWS)

    @pl.when(step == 0)
    def _():
        dk[...] = jnp.zeros_like(dk)
        dv[...] = jnp.zeros_like(dv)
        for g in range(KV_HEADS):
            kt[g] = jnp.transpose(k_ref[g].astype(f32)).astype(bf16)

    key_token = cols_ref[:, 0:1]
    token, begin = rows_ref[0:1, pl.ds(start, ROWS)], rows_ref[1:2, pl.ds(start, ROWS)]
    bias[...] = jnp.where((key_token <= token) & (key_token >= begin), 0.0, masked_score)
    scale = 1.0 / math.sqrt(HEAD_DIM)
    cos, sin = cos_t_ref[...] * scale, sin_t_ref[...] * scale
    for first in range(0, HEADS, 2):
        count = min(2, HEADS - first)
        grads = do_ref[rows, first * HEAD_DIM : (first + count) * HEAD_DIM]
        outs = []
        for n in range(first, first + count):
            g = n // GROUP
            q = q_ref[n, rows, :]
            do = grads[:, (n - first) * HEAD_DIM : (n - first + 1) * HEAD_DIM]
            s = matmul(k_ref[g], q, ((1,), (1,))) + bias[...]
            p = jnp.exp(s - lse_ref[n : n + 1, :])
            dp = matmul(v_ref[g], do, ((1,), (1,)))
            dv[g] += matmul(p.astype(bf16), do, ((1,), (0,)))
            pd = p * dp
            ds = (pd - p * jnp.sum(pd, axis=0, keepdims=True)).astype(bf16)
            dk[g] += matmul(ds, q, ((1,), (0,)))
            dq = matmul(kt[g], ds, ((1,), (0,)))
            outs.append(dq * cos - jnp.concatenate([dq[HALF:], dq[:HALF]], axis=0) * sin)
        out_ref[rows, first * HEAD_DIM : (first + count) * HEAD_DIM] = jnp.transpose(
            jnp.concatenate(outs, axis=0)
        ).astype(bf16)

    @pl.when(step == pl.num_programs(0) - 1)
    def _():
        cos, sin = cos_ref[:, :HEAD_DIM], sin_ref[:, :HEAD_DIM]
        for g in range(KV_HEADS):
            grad = dk[g]
            out_ref[:, QW + g * HEAD_DIM : QW + (g + 1) * HEAD_DIM] = (
                grad * cos - swap_halves(grad) * sin
            ).astype(bf16)
            out_ref[:, QW + KW + g * HEAD_DIM : QW + KW + (g + 1) * HEAD_DIM] = dv[g].astype(bf16)


def attend_bwd(q, k, v, lse, grad, cos, sin, cos_t, sin_t, cols, rows):
    count = grad.shape[0]
    whole = lambda *shape: pl.BlockSpec(shape, lambda i: (0,) * len(shape))
    return pl.pallas_call(
        attend_bwd_kernel,
        grid=(count // ROWS,),
        out_shape=jax.ShapeDtypeStruct((count, QW + 2 * KW), bf16),
        in_specs=[
            whole(HEADS, count, HEAD_DIM),
            whole(KV_HEADS, count, HEAD_DIM),
            whole(KV_HEADS, count, HEAD_DIM),
            pl.BlockSpec((16, ROWS), lambda i: (0, i)),
            whole(count, QW),
            whole(count, 2 * HEAD_DIM),
            whole(count, 2 * HEAD_DIM),
            pl.BlockSpec((HEAD_DIM, ROWS), lambda i: (0, i)),
            pl.BlockSpec((HEAD_DIM, ROWS), lambda i: (0, i)),
            whole(count, 2),
            whole(2, count),
        ],
        out_specs=whole(count, QW + 2 * KW),
        scratch_shapes=[
            pltpu.VMEM((count, ROWS), f32),
            pltpu.VMEM((KV_HEADS, count, HEAD_DIM), f32),
            pltpu.VMEM((KV_HEADS, count, HEAD_DIM), f32),
            pltpu.VMEM((KV_HEADS, HEAD_DIM, count), bf16),
        ],
        compiler_params=pltpu.CompilerParams(vmem_limit_bytes=56 << 20),
        name="attend_bwd",
    )(q, k, v, lse, grad, cos, sin, cos_t, sin_t, cols, rows)


def inverse_rms(values):
    return lax.rsqrt(jnp.mean(values * values, axis=-1, keepdims=True) + norm_eps)


def norm_back(values, gain, grad):
    scale = inverse_rms(values)
    unit = values * scale
    grad_unit = grad * gain
    grad_values = (grad_unit - unit * jnp.mean(grad_unit * unit, axis=-1, keepdims=True)) * scale
    return grad_values, jnp.sum(grad * unit, axis=0)


def forward_step(rows_in, tables, weights, section):
    wqkv, wo, wg, wu, wd, gain_attn, gain_ffn, router = weights
    normed = (rows_in * inverse_rms(rows_in) * gain_attn).astype(bf16)
    qkv = dot("kd,de->ke", normed, wqkv)
    mixed, q, k, v, lse = attend_fwd(qkv, *tables)
    attn = dot("ke,ed->kd", mixed, wo)
    middle = rows_in + attn
    inner = (middle * inverse_rms(middle) * gain_ffn).astype(bf16)
    gate = dot("kd,df->kf", inner, wg)
    up = dot("kd,df->kf", inner, wu)
    activated = (gate * jax.nn.sigmoid(gate) * up).astype(bf16)
    ffn = dot("kf,fd->kd", activated, wd)
    gate_c = jax.nn.sigmoid(jnp.sum(rows_in * router[:, section][None, :], axis=1, keepdims=True))
    branches = attn + ffn
    out = rows_in + gate_c * branches
    kept = (rows_in, normed, q, k, v, lse, mixed, middle, inner, gate.astype(bf16), up.astype(bf16), activated, gate_c, branches)
    return out, kept


def backward_step(grad_new, kept, tables, weights, section):
    wqkv, wo, wg, wu, wd, gain_attn, gain_ffn, router = weights
    rows_in, normed, q, k, v, lse, mixed, middle, inner, gate, up, activated, gate_c, branches = kept
    gate, up = gate.astype(f32), up.astype(f32)
    dz = jnp.sum(grad_new * branches, axis=1, keepdims=True) * gate_c * (1.0 - gate_c)
    router_grad = jnp.sum(rows_in * dz, axis=0)
    grad_rows = grad_new + dz * router[:, section][None, :]
    grad_branch = gate_c * grad_new
    grad_ffn = grad_branch.astype(bf16)
    grad_act = dot("kd,fd->kf", grad_ffn, wd)
    sig = jax.nn.sigmoid(gate)
    grad_gate = (grad_act * up * (sig + gate * sig * (1.0 - sig))).astype(bf16)
    grad_up = (grad_act * (gate * sig)).astype(bf16)
    grad_inner = dot("kf,df->kd", grad_gate, wg) + dot("kf,df->kd", grad_up, wu)
    grad_middle, gain_ffn_grad = norm_back(middle, gain_ffn, grad_inner)
    grad_attn = (grad_branch + grad_middle).astype(bf16)
    grad_mixed = dot("kd,ed->ke", grad_attn, wo).astype(bf16)
    grad_qkv = attend_bwd(q, k, v, lse, grad_mixed, *tables)
    grad_normed = dot("ke,de->kd", grad_qkv, wqkv)
    grad_norm_rows, gain_attn_grad = norm_back(rows_in, gain_attn, grad_normed)
    grad_rows = grad_rows + grad_middle + grad_norm_rows
    pairs = ((activated, grad_ffn), (inner, grad_gate), (inner, grad_up), (mixed, grad_attn), (normed, grad_qkv))
    return grad_rows, pairs, (gain_attn_grad, gain_ffn_grad, router_grad)


MESH = pl.DeviceIdType.MESH
GATHER_ORDER = (0, 1, 2, 3)


def place():
    d, z = lax.axis_index("dp"), lax.axis_index("fsdp")
    c, x, y = lax.rem(d, 2), lax.rem(lax.div(d, 2), 2), lax.div(d, 4)
    ids = dict(
        core={"dp": d + 1 - 2 * c},
        x={"dp": d + 2 - 4 * x},
        y={"dp": d + 4 - 8 * y},
        up={"fsdp": z + 1},
        down={"fsdp": z - 1},
    )
    return z, c, x, y, ids


def greet(z, ids):
    barrier = pltpu.get_barrier_semaphore()
    for name in ("core", "x", "y"):
        pl.semaphore_signal(barrier, inc=1, device_id=ids[name], device_id_type=MESH)

    @pl.when(z < 3)
    def _():
        pl.semaphore_signal(barrier, inc=1, device_id=ids["up"], device_id_type=MESH)

    @pl.when(z > 0)
    def _():
        pl.semaphore_signal(barrier, inc=1, device_id=ids["down"], device_id_type=MESH)

    pl.semaphore_wait(barrier, 5 - lax.div(z, 3) - lax.div(3 - z, 3))


def remote(src, dst, send, recv, target):
    return pltpu.make_async_remote_copy(
        src_ref=src, dst_ref=dst, send_sem=send, recv_sem=recv, device_id=target, device_id_type=MESH
    )


def piece(ref, a, lead, p, parts=4):
    if a < 3:
        width = ref.shape[-1] // parts
        return ref.at[(*lead, slice(None), pl.ds(pl.multiple_of(p * width, 128), width))]
    height = ref.shape[-2] // parts
    return ref.at[(*lead, pl.ds(pl.multiple_of(p * height, 16), height), slice(None))]


def pieces_of(a, x, y):
    f, s, wf, ws = (y, x, 2, 1) if a < 2 else (x, y, 2, 1)
    own = 2 * f + s
    nx = 2 * f + 1 - s if a < 2 else 2 * (1 - f) + s
    ny = 2 * (1 - f) + s if a < 2 else 2 * f + 1 - s
    return own, nx, ny, 2 * (1 - f) + 1 - s


def plane_stage(stage, refs, a, slot, lead, where, send, recv):
    z, c, x, y, ids = where
    own, nx, ny, far = pieces_of(a, x, y)
    first = [(own, "x", 0), (own, "y", 1), (own, "core", 3)]
    second = [(nx, "core", 4), (ny, "core", 5), (ny, "x", 2) if a < 2 else (nx, "y", 2)]
    third = [(far, "core", 6)]

    def copy(p, name, kind):
        part = piece(refs[a], a, lead, p)
        return remote(part, part, send.at[kind, a, slot], recv.at[kind, a, slot], ids[name])

    def arrived(p, kind):
        part = piece(refs[a], a, lead, p)
        remote(part, part, send.at[kind, a, slot], recv.at[kind, a, slot], ids["core"]).wait_recv()

    if stage == 1:
        for item in first:
            copy(*item).start()
    elif stage == 2:
        arrived(nx, 0)
        copy(*second[0]).start()
        arrived(ny, 1)
        copy(*second[1]).start()
        copy(*second[2]).start()
    elif stage == 3:
        arrived(far, 2)
        copy(*third[0]).start()
    else:
        other = (*lead[:-1], 1 - c)
        for p, kind in ((own, 3), (nx, 4), (ny, 5), (far, 6)):
            part = piece(refs[a], a, other, p)
            remote(part, part, send.at[kind, a, slot], recv.at[kind, a, slot], ids["core"]).wait_recv()
        for item in first + second + third:
            copy(*item).wait_send()


def gather_kernel(s0, s1, s2, s3, small, o0, o1, o2, o3, small_out, send, recv, zsend, zrecv, local):
    where = place()
    z, c, x, y, ids = where
    shards, outs = (s0, s1, s2, s3), (o0, o1, o2, o3)
    greet(z, ids)

    def along(a, origin, way):
        if a == 4:
            dst = small_out.at[origin]
            src = dst
        else:
            dst = src = piece(outs[a], a, (origin, c), pieces_of(a, x, y)[0])
        way_index = 0 if way == "up" else 1
        return src, dst, zsend.at[way_index, a, origin], zrecv.at[a, origin], ids[way]

    def own_copy(a, way):
        src, dst, ss, rs, target = along(a, z, way)
        src = small if a == 4 else piece(shards[a], a, (c,), pieces_of(a, x, y)[0])
        return remote(src, dst, ss, rs, target)

    kinds = (4,) + GATHER_ORDER

    @pl.when(z < 3)
    def _():
        for a in kinds:
            own_copy(a, "up").start()

    @pl.when(z > 0)
    def _():
        for a in kinds:
            own_copy(a, "down").start()

    def own_local(a):
        if a == 4:
            return pltpu.make_async_copy(small, small_out.at[z], local.at[a])
        return pltpu.make_async_copy(shards[a], outs[a].at[z], local.at[a])

    for a in kinds:
        own_local(a).start()

    def foreign(step, a, stage):
        for way, origin, there, more in (
            ("up", z - step, z >= step, z < 3),
            ("down", z + step, z <= 3 - step, z > 0),
        ):

            @pl.when(there)
            def _():
                if stage == 1:
                    remote(*along(a, origin, way)).wait_recv()

                    @pl.when(more)
                    def _():
                        remote(*along(a, origin, way)).start()

                if a < 4:
                    plane_stage(stage, outs, a, origin, (origin, c), where, send, recv)
                if stage == 4:

                    @pl.when(more)
                    def _():
                        remote(*along(a, origin, way)).wait_send()

    for step in (1, 2, 3):
        foreign(step, 4, 1)
    events = [(step, a) for step in (1, 2, 3) for a in GATHER_ORDER]
    for k in range(len(events) + 4):
        if k < len(events):
            foreign(*events[k], 1)
        if 2 <= k < len(events) + 2:
            foreign(*events[k - 2], 2)
        if 4 <= k:
            foreign(*events[k - 4], 3)
    for a in kinds:
        for step in (1, 2, 3):
            foreign(step, a, 4)

    @pl.when(z < 3)
    def _():
        for a in kinds:
            own_copy(a, "up").wait_send()

    @pl.when(z > 0)
    def _():
        for a in kinds:
            own_copy(a, "down").wait_send()

    for a in kinds:
        own_local(a).wait()


def gather_weights(shards, small):
    dma = pltpu.SemaphoreType.DMA
    vmem, hbm = pl.BlockSpec(memory_space=pltpu.VMEM), pl.BlockSpec(memory_space=pl.ANY)
    halves = [s.reshape(2, s.shape[0] // 2, s.shape[1]) for s in shards]
    out = pl.pallas_call(
        gather_kernel,
        out_shape=tuple(jax.ShapeDtypeStruct((4, *s.shape), s.dtype) for s in halves + [small]),
        in_specs=[vmem] * 5,
        out_specs=[hbm] * 5,
        scratch_shapes=[dma((7, 4, 4)), dma((7, 4, 4)), dma((2, 5, 4)), dma((5, 4)), dma((5,))],
        compiler_params=pltpu.CompilerParams(collective_id=0, has_side_effects=True, vmem_limit_bytes=32 << 20),
        name="gather_weights",
    )(*halves, small)
    return [o.reshape(-1, o.shape[-1]) for o in out[:4]], out[4]


TARGETS = (3, 0, 2, 1)


def add_into(dst, dlead, drow, dcol, src, slead, rows, cols):
    wide = cols % 640 == 0
    count = cols // 640 if wide else rows // 80

    def one(i):
        if wide:
            shift = pl.multiple_of(i * 640, 128)
            at_src = (*slead, slice(None), pl.ds(shift, 640))
            at_dst = (*dlead, slice(None), pl.ds(pl.multiple_of(dcol + shift, 128), 640))
        else:
            shift = pl.multiple_of(i * 80, 16)
            at_src = (*slead, pl.ds(shift, 80), slice(None))
            at_dst = (*dlead, pl.ds(pl.multiple_of(drow + shift, 16), 80), slice(None))
        dst[at_dst] = (dst[at_dst].astype(f32) + src[at_src].astype(f32)).astype(dst.dtype)

    if count == 1:
        one(0)
    else:

        @pl.loop(0, count)
        def _(i):
            one(i)


def reduce_kernel(
    g0, g1, g2, g3, small, o0, o1, o2, o3, small_out,
    a0, a1, a2, a3, c0, c1, c2, c3, p0, p1, p2, p3, q0, q1, q2, q3, u0, u1, u2, u3, d0, d1, d2, d3,
    small_in, small_out_buf, csend, crecv, psend, precv, zsend, zrecv, send, recv, loads, ssend, srecv,
):
    where = place()
    z, c, x, y, ids = where
    full, outs, acc, cbuf = (g0, g1, g2, g3), (o0, o1, o2, o3), (a0, a1, a2, a3), (c0, c1, c2, c3)
    first, second = (p0, p1, p2, p3), (q0, q1, q2, q3)
    up, down = (u0, u1, u2, u3), (d0, d1, d2, d3)
    greet(z, ids)

    def load(a, t):
        return pltpu.make_async_copy(full[a].at[t, c], acc[a].at[t], loads.at[a, t])

    def core_copy(a, t):
        return remote(full[a].at[t, 1 - c], cbuf[a].at[t], csend.at[a, t], crecv.at[a, t], ids["core"])

    def coords(a):
        return (y, x, "y", "x") if a < 2 else (x, y, "x", "y")

    def first_copy(a, t):
        f, s, nf, ns = coords(a)
        return remote(piece(acc[a], a, (t,), 1 - f, 2), first[a].at[t], psend.at[0, a, t], precv.at[0, a, t], ids[nf])

    def second_copy(a, t):
        f, s, nf, ns = coords(a)
        return remote(
            piece(acc[a], a, (t,), 2 * f + 1 - s), second[a].at[t], psend.at[1, a, t], precv.at[1, a, t], ids[ns]
        )

    def own_piece(a, t):
        f, s, nf, ns = coords(a)
        return piece(acc[a], a, (t,), 2 * f + s)

    def up_copy(a, t):
        return remote(own_piece(a, t), up[a].at[t], zsend.at[0, a, t], zrecv.at[0, a, t], ids["up"])

    def down_copy(a, t):
        return remote(own_piece(a, t), down[a].at[t], zsend.at[1, a, t], zrecv.at[1, a, t], ids["down"])

    def add_piece(a, t, src, index, parts):
        rows, cols = src.shape[-2:]
        offset = index * (acc[a].shape[-1] // parts if a < 3 else acc[a].shape[-2] // parts)
        add_into(acc[a], (t,), 0 if a < 3 else offset, offset if a < 3 else 0, src, (t,), rows, cols)

    def stage2(t):
        for a in range(4):
            load(a, t).wait()
            core_copy(a, t).wait_recv()
            add_piece(a, t, cbuf[a], 0, 1)
            first_copy(a, t).start()

    def stage3(t):
        for a in range(4):
            first_copy(a, t).wait_recv()
            add_piece(a, t, first[a], coords(a)[0], 2)
            second_copy(a, t).start()

    def own_index(a):
        f, s, nf, ns = coords(a)
        return 2 * f + s

    def stage4(t):
        for a in range(4):
            second_copy(a, t).wait_recv()
            add_piece(a, t, second[a], own_index(a), 4)

            if t > 0:

                @pl.when(z == 0)
                def _():
                    up_copy(a, t).start()

            if t < 3:

                @pl.when(z == 3)
                def _():
                    down_copy(a, t).start()

    def stage5(t, level):
        for a in range(4):
            if 0 < level <= t:
                up_copy(a, t).wait_recv()
                add_piece(a, t, up[a], own_index(a), 4)
                if level < t:
                    up_copy(a, t).start()
            if t <= level < 3:
                down_copy(a, t).wait_recv()
                add_piece(a, t, down[a], own_index(a), 4)
                if level > t:
                    down_copy(a, t).start()

    def small_copy(k, name):
        return remote(small_out_buf.at[k], small_in.at[k], ssend.at[k], srecv.at[k], ids[name])

    def small_step(k, name):
        small_copy(k, name).wait_recv()
        small_out[...] = small_out[...] + small_in[k]

    def small_send(k, name):
        small_out_buf[k] = small_out[...]
        small_copy(k, name).start()

    small_out[...] = small[...]
    small_send(0, "core")
    for t in TARGETS:
        for a in range(4):
            core_copy(a, t).start()
            load(a, t).start()
    small_step(0, "core")
    small_send(1, "x")
    small_step(1, "x")
    small_send(2, "y")

    n = len(TARGETS)
    turns = {3: [(3, 1)], 4: [(3, 2), (0, 2)], 5: [(3, 3), (0, 1), (2, 1)], 6: [(0, 0), (2, 2), (1, 2)], 7: [(1, 1)]}
    for k in range(n + 4):
        if k < n:
            stage2(TARGETS[k])
        if 1 <= k < n + 1:
            stage3(TARGETS[k - 1])
        if 2 <= k < n + 2:
            stage4(TARGETS[k - 2])
        for t, level in turns.get(k, ()):

            @pl.when(z == level)
            def _():
                stage5(t, level)

    small_step(2, "y")

    small_out_buf[3] = small_out[...]
    small_out_buf[4] = small_out[...]

    @pl.when(z > 0)
    def _():
        small_copy(3, "up").wait_recv()
        small_out_buf[3] = small_out_buf[3] + small_in[3]

    @pl.when(z < 3)
    def _():
        small_copy(3, "up").start()
        small_copy(4, "down").wait_recv()
        small_out_buf[4] = small_out_buf[4] + small_in[4]

    @pl.when(z > 0)
    def _():
        small_copy(4, "down").start()

    small_out[...] = small_out_buf[3] + small_out_buf[4] - small_out[...]

    for a in range(4):
        src = own_piece(a, z)
        dst = piece(outs[a], a, (c,), own_index(a))
        dst[...] = src[...]
        plane_stage(1, outs, a, 0, (c,), where, send, recv)
    for stage in (2, 3, 4):
        for a in range(4):
            plane_stage(stage, outs, a, 0, (c,), where, send, recv)

    for k, name in enumerate(("core", "x", "y")):
        small_copy(k, name).wait_send()

    @pl.when(z < 3)
    def _():
        small_copy(3, "up").wait_send()

    @pl.when(z > 0)
    def _():
        small_copy(4, "down").wait_send()

    for t in range(4):
        for a in range(4):
            core_copy(a, t).wait_send()
            first_copy(a, t).wait_send()
            second_copy(a, t).wait_send()
            if t > 0:

                @pl.when(z < t)
                def _():
                    up_copy(a, t).wait_send()

            if t < 3:

                @pl.when(z > t)
                def _():
                    down_copy(a, t).wait_send()


def reduce_grads(grads, small):
    dma = pltpu.SemaphoreType.DMA
    vmem, hbm = pl.BlockSpec(memory_space=pltpu.VMEM), pl.BlockSpec(memory_space=pl.ANY)
    full = [g.reshape(4, 2, g.shape[0] // 8, g.shape[1]) for g in grads]

    def buffers(parts):
        shapes = []
        for a, g in enumerate(full):
            rows, cols = g.shape[2:]
            shapes.append((4, rows, cols // parts) if a < 3 else (4, rows // parts, cols))
        return [pltpu.VMEM(s, bf16) for s in shapes]

    out = pl.pallas_call(
        reduce_kernel,
        out_shape=tuple(jax.ShapeDtypeStruct(g.shape[1:], bf16) for g in full)
        + (jax.ShapeDtypeStruct(small.shape, f32),),
        in_specs=[hbm] * 4 + [vmem],
        out_specs=[vmem] * 5,
        scratch_shapes=buffers(1) + buffers(1) + buffers(2) + buffers(4) + buffers(4) + buffers(4)
        + [pltpu.VMEM((5, *small.shape), f32)] * 2
        + [dma((4, 4)), dma((4, 4)), dma((2, 4, 4)), dma((2, 4, 4)), dma((2, 4, 4)), dma((2, 4, 4))]
        + [dma((7, 4, 1)), dma((7, 4, 1)), dma((4, 4)), dma((5,)), dma((5,))],
        compiler_params=pltpu.CompilerParams(collective_id=1, has_side_effects=True, vmem_limit_bytes=60 << 20),
        name="reduce_grads",
    )(*full, small)
    return [o.reshape(-1, o.shape[-1]) for o in out[:4]], out[4]


def gather_all(shard):
    if shard.shape[0] % lax.axis_size("dp"):
        return lax.all_gather(shard, "fsdp", axis=0, tiled=True)
    rows = shard.shape[0] // lax.axis_size("dp")
    part = lax.dynamic_slice_in_dim(shard, lax.axis_index("dp") * rows, rows, 0)
    return lax.all_gather(part, ("fsdp", "dp"), axis=0, tiled=True)


def reduce_all(total):
    chunks = lax.axis_size("dp") * lax.axis_size("fsdp")
    if total.shape[0] % chunks:
        part = lax.psum_scatter(total, "fsdp", scatter_dimension=0, tiled=True)
        return lax.psum(part, "dp")
    rows = total.shape[0] // chunks
    padded = jnp.pad(total.reshape(chunks, rows, -1), ((0, 0), (0, -rows % 16), (0, 0)))
    part = lax.psum_scatter(padded.reshape(-1, total.shape[1]), ("fsdp", "dp"), scatter_dimension=0, tiled=True)[:rows]
    return lax.all_gather(part, "dp", axis=0, tiled=True)


def body(
    inputs, w_query, w_key, w_value, w_out, w_gate, w_up, w_down, gain_attn, gain_ffn, w_router,
    seq_start, pick_first, pick_second, pick_third, out_grad,
):
    picks = (pick_first, pick_second, pick_third)
    counts = tuple(p.shape[0] for p in picks)
    tokens = inputs.shape[0]

    by_kernel = lax.axis_size("dp") == 8 and lax.axis_size("fsdp") == 4
    owned = gain_attn.shape[0]
    first = jnp.concatenate([w_out, w_query, w_key, w_value], axis=1)
    small = jnp.concatenate([gain_attn[None], gain_ffn[None], w_router.T], axis=0)
    if by_kernel:
        small = jnp.pad(small, ((0, 16 - small.shape[0]), (0, -owned % 128)))
        (first, wg, wu, wd), small = gather_weights([first, w_gate, w_up, w_down], small)
        small = small[:, :, :owned].transpose(1, 0, 2).reshape(16, -1).astype(f32)
    else:
        first, wg, wu, wd = gather_all(first), gather_all(w_gate), gather_all(w_up), gather_all(w_down)
        small = lax.all_gather(small, "fsdp", axis=1, tiled=True).astype(f32)
    wo, wqkv = first[:, :QW], first[:, QW:]
    weights = (wqkv, wo, wg, wu, wd, small[0], small[1], small[2 : 2 + NREC].T)

    places = jnp.arange(tokens, dtype=jnp.int32)
    level = jnp.full((tokens,), NREC, jnp.int32)
    for p in picks:
        level = level - jnp.any(p[:, None] == places[None, :], axis=0).astype(jnp.int32)
    kinds = level[None, :] == jnp.arange(NREC + 1, dtype=jnp.int32)[:, None]
    before = (places[:, None] < places[None, :]).astype(bf16)
    ahead = dot("ct,tu->cu", kinds.astype(bf16), before).astype(jnp.int32)
    bases = jnp.array([0, counts[2], counts[1], counts[0]], jnp.int32)
    position = jnp.sum(jnp.where(kinds, ahead + bases[:, None], 0), axis=0)
    chosen = position[None, :] == places[:, None]
    order = chosen.astype(bf16)
    token = jnp.sum(jnp.where(chosen, places[None, :], 0), axis=1)
    begin = jnp.sum(jnp.where(chosen, seq_start[None, :], 0), axis=1)
    frequency = jnp.exp(jnp.arange(HALF, dtype=f32) * (-2.0 * math.log(10000.0) / HEAD_DIM))
    angles = (token - begin).astype(f32)[:, None] * frequency[None, :]
    cos, sin = jnp.cos(angles), jnp.sin(angles)
    cos = jnp.concatenate([cos] * 4, axis=1)
    sin = jnp.concatenate([-sin, sin] * 2, axis=1)
    cos_t, sin_t = cos[:, :HEAD_DIM].T, sin[:, :HEAD_DIM].T
    rows2 = jnp.stack([token, begin]).astype(f32)
    cols2 = jnp.stack([token, begin], axis=1).astype(f32)
    tables = [(cos[:k], sin[:k], cos_t[:, :k], sin_t[:, :k], cols2[:k], rows2[:, :k]) for k in counts]

    hidden = dot("pt,td->pd", order, inputs)
    grads = dot("pt,td->pd", order, out_grad)

    kept, news, rows_in = [], [], hidden[: counts[0]]
    for r in range(NREC):
        new, saved = forward_step(rows_in, tables[r], weights, r)
        kept.append(saved)
        news.append(new)
        if r + 1 < NREC:
            rows_in = new[: counts[r + 1]]
    final = jnp.concatenate(
        [
            news[2].astype(bf16),
            news[1][counts[2] :].astype(bf16),
            news[0][counts[1] :].astype(bf16),
            hidden[counts[0] :].astype(bf16),
        ],
        axis=0,
    )
    result = dot("pt,pd->td", order, final).astype(bf16)

    grad_new = grads[: counts[2]]
    pairs, smalls = [], []
    for r in reversed(range(NREC)):
        grad_rows, step_pairs, step_small = backward_step(grad_new, kept[r], tables[r], weights, r)
        pairs.append(step_pairs)
        smalls.append(step_small)
        if r > 0:
            grad_new = jnp.concatenate([grad_rows, grads[counts[r] : counts[r - 1]]], axis=0)
    grad_final = jnp.concatenate([grad_rows.astype(bf16), grads[counts[0] :].astype(bf16)], axis=0)
    grad_inputs = dot("pt,pd->td", order, grad_final).astype(bf16)

    sums = []
    for i in range(5):
        left = jnp.concatenate([p[i][0] for p in pairs], axis=0)
        right = jnp.concatenate([p[i][1] for p in pairs], axis=0)
        sums.append(dot("kd,ke->de", left, right).astype(bf16))
    down, gate, up, out, qkv = sums
    first = jnp.concatenate([out, qkv], axis=1)
    small = jnp.stack(
        [smalls[0][0] + smalls[1][0] + smalls[2][0], smalls[0][1] + smalls[1][1] + smalls[2][1]]
        + [s[2] for s in reversed(smalls)]
    )
    if by_kernel:
        small = jnp.pad(small, ((0, 8 - small.shape[0]), (0, -small.shape[1] % 128)))
        (first, gate, up, down), small = reduce_grads([first, gate, up, down], small)
        small = lax.dynamic_slice_in_dim(small, lax.axis_index("fsdp") * owned, owned, 1)
    else:
        first, gate, up, down = reduce_all(first), reduce_all(gate), reduce_all(up), reduce_all(down)
        small = lax.psum_scatter(small, "fsdp", scatter_dimension=1, tiled=True)
        small = lax.psum(small, "dp")
    first = first.astype(f32)
    return (
        result,
        grad_inputs,
        first[:, QW : 2 * QW],
        first[:, 2 * QW : 2 * QW + KW],
        first[:, 2 * QW + KW :],
        first[:, :QW],
        gate.astype(f32),
        up.astype(f32),
        down.astype(f32),
        small[0],
        small[1],
        small[2 : 2 + NREC].T,
    )


def solution(mesh):
    tok, row = P(("dp", "fsdp")), P("fsdp")
    in_specs = (tok,) + (row,) * 10 + (tok,) * 5
    out_specs = (tok, tok) + (row,) * 10
    return jax.shard_map(body, mesh=mesh, in_specs=in_specs, out_specs=out_specs, check_vma=False)
```
